32 devices in a mesh: con: 16 (over z, y, x), rep: 2 (over core).
Axes of the slice: x: 2, y: 2, z: 4, core: 2. Of those that a mesh axis runs over, the one named last changes fastest.
Arguments:
- tamps: bfloat16 [16384, 14336], P('rep', 'con'), may hold values from -6 to 6
- integrals: bfloat16 [1024, 16384], P('con', 'rep'), may hold values from -0.0625 to 0.0625
Outputs:
- ladder: bfloat16 [1024, 14336], P('rep', 'con')
The draws below stay inside these ranges and needn't reach their ends.
All inputs are finite; a program needn't handle non-finite values.
Results may differ from the reference program's by a relative error of at most 0.001.
Values may be sent and summed in bfloat16 or wider, within the bound.
A program may use at most 128 MiB of HBM per device.

```python
import jax
import jax.numpy as jnp
from jax import lax

CD = 16384
AB = 1024
OO = 14336


def raised(drawn, stream_key, source, target, parts, factor):
    def block_of(dim):
        return (jnp.arange(drawn.shape[dim]) // (drawn.shape[dim] // parts)).reshape((-1,) + (1,) * (drawn.ndim - 1 - dim))

    near = jax.random.permutation(stream_key, parts)[block_of(target)]
    far = (block_of(target) + parts // 2) % parts
    return jnp.where((block_of(source) == near) | (block_of(source) == far), factor * drawn, drawn)


def block_levels(own_key, extent, pieces, smallest, top_value):
    gain = 1.0
    for dim, blocks in pieces:
        draws = jax.random.uniform(jax.random.fold_in(jax.random.fold_in(own_key, 6), dim), (blocks,), jnp.float32, smallest / len(pieces), top_value / len(pieces))
        gain = gain * jnp.repeat(jnp.exp(draws), extent[dim] // blocks).reshape((-1,) + (1,) * (len(extent) - 1 - dim))
    return gain


def noise(rng, dims, deviation, most, shards=(), kind=jnp.bfloat16):
    entries = deviation * jax.random.normal(rng, dims, jnp.float32)
    if shards:
        entries = entries * block_levels(rng, dims, shards, -0.22, 0.18)
    return jnp.clip(entries, -most, most).astype(kind)


def bell_draw_with(own_key, shape, spread, bound, cuts, heavy, dtype=jnp.bfloat16):
    drawn = spread * jax.random.normal(own_key, shape, jnp.float32)
    if cuts:
        drawn = drawn * block_levels(own_key, shape, cuts, -0.22, 0.18)
    return jnp.clip(raised(drawn, jax.random.fold_in(own_key, 3), *heavy), -bound, bound).astype(dtype)


def setup_inputs(seed: int = 0) -> dict:
    arg_keys = jax.random.split(jax.random.key(seed), 3)
    return {
        "tamps": noise(arg_keys[0], (CD, OO), 1.0, 6.0, ((0, 2), (1, 16))),
        "integrals": bell_draw_with(arg_keys[1], (AB, CD), CD ** -0.5, 0.0625, ((0, 16), (1, 2)), (1, 0, 16, 2.0)),
    }


def reference(tamps, integrals):
    left = integrals.astype(jnp.float32)
    total = tamps.shape[1]
    width = 1024
    count = total // width
    if total % width != 0:
        width = total
        count = 1
    blocks = jnp.transpose(tamps.reshape(tamps.shape[0], count, width), (1, 0, 2))

    def one_block(piece):
        return jnp.dot(left, piece.astype(jnp.float32), preferred_element_type=jnp.float32)

    contracted = lax.map(one_block, blocks)
    contracted = jnp.transpose(contracted, (1, 0, 2)).reshape(integrals.shape[0], total)
    return contracted.astype(jnp.bfloat16)
```

```python
import functools

import jax
import jax.numpy as jnp
from jax import lax
from jax.experimental import pallas as pl
from jax.experimental.pallas import tpu as pltpu
from jax.sharding import PartitionSpec as P

MESH = pl.DeviceIdType.MESH

HELPED, PLAIN = 2, 5
HELPED_WIDE, PLAIN_WIDE = 7, 10
CHUNKS = HELPED + PLAIN
PER_BLOCK = 4
BLOCKS = 7
SENT_LAG = 5
AMPS_THERE = 5
SUM_LAG = 1
PIECES = 16 * CHUNKS
AMPS = PIECES
SUMS = AMPS + BLOCKS * PER_BLOCK
NONE = 255

END_X = (
    2, 3, 6, -1, 62, 11, -1, 61, 67, -1, 59, 20, 4, -1, 19, 66, -1, 41, 75, -1, 102, 97, 107, -1,
    27, 46, -1, 51, 72, -1, 88, 111, 17, -1, 108, 9, -1, 73, 109, -1, 53,
)
END_Y = (
    2, 6, 5, -1, 11, 30, -1, 3, 10, -1, 89, 40, 12, -1, 19, 26, -1, 41, 48, -1, 102, 32, 107, -1,
    16, 94, -1, 55, 20, -1, 52, 54, 100, -1, 17, -1, 109, 80, -1, 37,
)
END_IN = (
    1, 0, 6, 5, 112, 113, 114, 115, 116, 117, 86, -1, 59, 118, 119, 120, 121, 122, 123, 124, 125,
    126, 127, 128, 88, -1, 129, 130, 131, 132, 133, 134, 135, 136, 137, 138, 139, 73, 80, -1, 110,
)
MID_X = (
    12, 8, 7, 13, 15, 11, -1, 5, 71, 21, 22, 56, 57, 42, 98, 78, 59, -1, 107, 102, -1, 104, 46, 62,
    -1, 27, 72, -1, 20, 88, -1, 10, 75, 31, -1, 109, 95, -1, 94, 32,
)
MID_Y = (
    9, 8, 7, 1, 36, 15, 35, 72, 0, 39, -1, 42, 49, 41, 84, 27, -1, 102, 86, -1, 87, 79, 107, -1, 19,
    58, -1, 90, 88, -1, 100, 52, 26, -1, 38, 103, -1, 45, 81, -1, 33,
)
MID_OUT = (
    11, 9, 10, -1, 20, 40, -1, 12, 65, -1, 26, 19, 41, -1, 54, 27, -1, 102, 107, -1, 16, 140, 141,
    142, 143, -1, 144, 52, 17, -1, 145, 146, 147, 109, 148, -1, 149, 150, 151, -1, 152, 153,
)
MID_IN = (
    13, 8, 12, 65, -1, 0, 5, 1, 35, 57, 33, -1, 6, 95, -1, 86, 50, 56, 97, 83, -1, 79, 10, -1, 31,
    76, -1, 90, 75, 88, -1, 100, 32, -1, 38, 44, -1, 82, 3, 103,
)
END_FROM_X = (
    -1, -1, -1, 30, 31, -1, 34, 90, -1, 39, 89, -1, 95, 87, 48, -1, 32, 47, -1, 94, 13, -1, 103, 74,
    69, -1, 79, 55, -1, 18, 23, -1, 100, 60, 83, -1, 45, 80, -1, 37, 101, -1, 81, 25,
)
END_FROM_Y = (
    -1, -1, -1, 58, 62, -1, 61, 67, -1, 86, 59, -1, 66, 33, 96, -1, 68, 75, -1, 82, 97, -1, 104, 46,
    88, -1, 51, 72, -1, 38, 111, -1, 76, 108, 110, -1, 44, 73, -1, 53, 24, -1, 93,
)
END_FROM_MID = (
    -1, -1, -1, 11, 9, -1, 10, 20, -1, 40, 12, -1, 65, 26, 19, -1, 41, 54, -1, 27, 102, -1, 107, 16,
    140, 141, 142, -1, 143, 144, 52, -1, 17, 145, 146, 147, 109, -1, 148, 149, 150, 151, -1, 152,
    153,
)
MID_FROM_X = (
    -1, -1, -1, 40, 36, 35, 41, 43, -1, 39, 33, 99, 49, 50, 84, 85, 14, 70, 106, -1, 87, 79, -1, 74,
    76, 18, -1, 90, 55, -1, 100, 48, -1, 60, 38, 103, -1, 3, 81, -1, 67, 66, -1, 4,
)
MID_FROM_Y = (
    -1, -1, -1, 65, 64, 63, 57, 92, 71, 91, 16, 56, -1, 95, 98, 105, 97, 28, -1, 83, 46, -1, 30, 31,
    23, -1, 51, 75, -1, 2, 34, -1, 32, 44, 108, -1, 82, 94, -1, 47, 101, -1, 25, 89,
)
MID_FROM_MID = (
    -1, -1, -1, 20, 15, 19, -1, 72, 21, 26, 22, 42, 78, -1, 54, 27, -1, 102, 107, 29, 77, 104, -1,
    62, 58, -1, 17, 52, -1, 69, 111, 68, -1, 109, 93, -1, 53, 45, -1, 37, 61, 24, -1, 96,
)
MID_FROM_END = (
    -1, -1, -1, 1, 0, 6, 5, 112, 113, 114, 115, 116, 117, -1, 86, 59, 118, 119, 120, 121, 122, 123,
    124, 125, 126, 127, 128, -1, 88, 129, 130, 131, 132, 133, 134, 135, 136, 137, 138, 139, 73, -1,
    80, 110,
)
END = (END_X, END_Y, END_IN, (-1,))
MID = (MID_X, MID_Y, MID_IN, MID_OUT)
END_FROM = (END_FROM_X, END_FROM_Y, END_FROM_MID, (-1,))
MID_FROM = (MID_FROM_X, MID_FROM_Y, MID_FROM_MID, MID_FROM_END)
SENDS = max(map(len, END + MID))
ROUNDS = max(map(len, END_FROM + MID_FROM))
X, Y, IN, OUT = range(4)


def parts(code):
    return code // CHUNKS // 4, code // CHUNKS % 4, code % CHUNKS


def arrivals(mid):
    there = {(0, 1 if mid else 0, c): 0 for c in range(CHUNKS)}
    amps, sums = {}, {}
    for table in MID_FROM if mid else END_FROM:
        for r, code in enumerate(table):
            if 0 <= code < PIECES:
                there[parts(code)] = r
            elif AMPS <= code < SUMS:
                amps[(code - AMPS) // PER_BLOCK] = r
            elif code >= SUMS:
                sums[(code - SUMS) // 2] = r
    return there, amps, sums


def plan(mid):
    there, amps, sums = arrivals(mid)
    ready = []
    for q in range(4):
        for c in range(0 if mid else HELPED, CHUNKS):
            ready.append((max(there[q, p, c] for p in range(4)), q, c))
    ready.sort()
    at, done, count = [], [], 0
    for r in range(AMPS_THERE, ROUNDS):
        room = 2 if r < ROUNDS - 1 else len(ready)
        while ready and room and ready[0][0] <= r:
            _, q, c = ready.pop(0)
            at.append((r, q * CHUNKS + c))
            room -= 1
    whole = [max(r for r, code in at if code // CHUNKS == q) for q in range(4)]
    helped_there = max(there[q, p, c] for q in range(4) for p in range(4) for c in range(HELPED)) if mid else 0
    blocks = []
    for j in range(BLOCKS):
        if mid:
            blocks.append(max(amps[j], helped_there, blocks[-1] + 1 if j else 0))
        else:
            blocks.append(sums[j])
    return at, whole, blocks


def chain(index, values):
    out = values[-1]
    for i in range(len(values) - 2, -1, -1):
        out = jnp.where(index == i, values[i], out)
    return out


def pick(mid, index, of_mid, of_end):
    size = max(len(of_mid), len(of_end))
    size += -size % 3
    words = []
    for table in (of_mid, of_end):
        full = [NONE if v < 0 else v for v in table] + [NONE] * (size - len(table))
        words.append([full[i] + 256 * full[i + 1] + 65536 * full[i + 2] for i in range(0, size, 3)])
    word = chain(index // 3, [a if a == b else jnp.where(mid, a, b) for a, b in zip(*words)])
    digit = index % 3
    shifted = jnp.where(digit == 0, word, jnp.where(digit == 1, word // 256, word // 65536))
    inside = jnp.logical_and(index >= 0, index < size)
    return jnp.where(inside, shifted % 256, NONE)


def kernel(
    tamps_hbm, slab_hbm, out_ref, helped, plain, amps, lent, total, other, part, inbox,
    send_sem, recv_sem, own_sem, amps_sem, col_send, col_recv, part_send, part_recv,
):
    me = lax.axis_index("con")
    core = lax.axis_index("rep")
    z, y, x = me // 4, (me // 2) % 2, me % 2
    rows = slab_hbm.shape[0]
    columns = amps.shape[1]
    half = 2 * rows
    own = y * 2 + x
    low = z < 2
    mid = jnp.logical_and(z > 0, z < 3)
    deep_helped, deep_plain = HELPED_WIDE * 128, PLAIN_WIDE * 128
    deep_all_helped = HELPED * deep_helped
    deep_part = deep_all_helped // PER_BLOCK

    def turned(q):
        qx, qy = q % 2, q // 2
        return (y + qy - 2 * y * qy) * 2 + (x + qx - 2 * x * qx)

    neighbour = (
        z * 4 + y * 2 + 1 - x,
        z * 4 + (1 - y) * 2 + x,
        jnp.where(low, me + 4, me - 4),
        jnp.where(low, me - 4, me + 4),
    )
    load_amps = [
        pltpu.make_async_copy(
            tamps_hbm.at[pl.ds(first, count), :], amps.at[pl.ds(first, count), :], amps_sem.at[k]
        )
        for k, (first, count) in enumerate(
            ((0, deep_all_helped), (deep_all_helped, PLAIN * deep_plain))
        )
    ]

    def load(c):
        here = pl.ds(pl.multiple_of((own * 4 + z) * rows, rows), rows)
        if c < HELPED:
            cut = slice(c * deep_helped, (c + 1) * deep_helped)
            return pltpu.make_async_copy(slab_hbm.at[:, cut], helped.at[c, here, :], own_sem.at[c])
        first = deep_all_helped + (c - HELPED) * deep_plain
        cut = slice(first, first + deep_plain)
        return pltpu.make_async_copy(slab_hbm.at[:, cut], plain.at[c - HELPED, here, :], own_sem.at[c])

    barrier = pltpu.get_barrier_semaphore()
    for way in (X, Y, IN):
        pl.semaphore_signal(barrier, inc=1, device_id=(neighbour[way], core), device_id_type=MESH)
    pl.semaphore_signal(barrier, inc=1, device_id=(me, 1 - core), device_id_type=MESH)

    @pl.when(mid)
    def _():
        pl.semaphore_signal(barrier, inc=1, device_id=(neighbour[OUT], core), device_id_type=MESH)

    for c in range(CHUNKS):
        load(c).start()
    pl.semaphore_wait(barrier, jnp.where(mid, 5, 4))
    for c in range(CHUNKS):
        load(c).wait()

    def remote(src, dst, way, r, arrival):
        return pltpu.make_async_remote_copy(
            src_ref=src,
            dst_ref=dst,
            send_sem=send_sem.at[way, r],
            recv_sem=recv_sem.at[arrival],
            device_id=(neighbour[way], core),
            device_id_type=MESH,
        )

    def message(act, code, way, r, amps_too, sums_too):
        q, p, c = parts(code)
        place = turned(q) * 4 + jnp.where(low, p, 3 - p)
        mine = pl.ds(pl.multiple_of(place * rows, rows), rows)
        is_piece = code < PIECES

        @pl.when(jnp.logical_and(is_piece, c < HELPED))
        def _():
            piece = helped.at[c, mine, :]
            act(remote(piece, piece, way, r, place * CHUNKS + c))

        @pl.when(jnp.logical_and(is_piece, c >= HELPED))
        def _():
            piece = plain.at[c - HELPED, mine, :]
            act(remote(piece, piece, way, r, place * CHUNKS + c))

        if amps_too is not None:

            @pl.when(jnp.logical_and(amps_too, jnp.logical_and(code >= AMPS, code < SUMS)))
            def _():
                k = code - AMPS
                j = k // PER_BLOCK
                deep = pl.ds(pl.multiple_of(k % PER_BLOCK * deep_part, deep_part), deep_part)
                cut = pl.ds(pl.multiple_of(j * 128, 128), 128)
                act(remote(tamps_hbm.at[deep, cut], lent.at[j, deep, :], way, r, code))

        if sums_too is not None:

            @pl.when(jnp.logical_and(sums_too, jnp.logical_and(code >= SUMS, code < NONE)))
            def _():
                k = code - SUMS
                two = pl.ds(k % 2 * 2, 2)
                act(remote(part.at[k // 2, core, two], inbox.at[k // 2, two], way, r, code))

    end = jnp.logical_not(mid)

    def outgoing(act, r):
        for way in range(4):
            code = pick(mid, r, MID[way], END[way])
            message(act, code, way, r, end if way == IN else None, mid if way == OUT else None)

    def incoming(r):
        for way in range(4):
            code = pick(mid, r, MID_FROM[way], END_FROM[way])
            message(
                lambda copy: copy.wait_recv(), code, way, 0,
                mid if way == OUT else None, end if way == IN else None,
            )

    mid_at, mid_whole, mid_blocks = plan(True)
    end_at, end_whole, end_blocks = plan(False)
    assert all(MID_OUT.index(SUMS + 2 * j) >= r + SUM_LAG for j, r in enumerate(mid_blocks))
    assert len(set(end_blocks)) == BLOCKS

    def count_of(at):
        return [sum(s <= r for s, _ in at) for r in range(ROUNDS)]

    def units(r):
        return pick(mid, r, count_of(mid_at), count_of(end_at))

    def multiply(left, column, first, deep):
        for start in range(0, columns, 256):
            cut = slice(start, min(start + 256, columns))
            total[column, :, cut] += jnp.dot(
                left, amps[pl.ds(first, deep), cut], preferred_element_type=jnp.float32
            )

    def product(code):
        column, c = turned(code // CHUNKS), code % CHUNKS
        mine = pl.ds(pl.multiple_of(column * 4 * rows, 4 * rows), 4 * rows)

        @pl.when(c < HELPED)
        def _():
            first = pl.multiple_of(c * deep_helped, 128)
            multiply(helped[c, mine, :], column, first, deep_helped)

        @pl.when(c >= HELPED)
        def _():
            first = pl.multiple_of(deep_all_helped + (c - HELPED) * deep_plain, 128)
            multiply(plain[c - HELPED, mine, :], column, first, deep_plain)

    def exchange(j):
        return pltpu.make_async_remote_copy(
            src_ref=part.at[j, 1 - core],
            dst_ref=inbox.at[j],
            send_sem=part_send.at[j],
            recv_sem=part_recv.at[j],
            device_id=(me, 1 - core),
            device_id_type=MESH,
        )

    def lend(j):
        def column(k, _):
            mine = pl.ds(pl.multiple_of(k * 4 * rows, 4 * rows), 4 * rows)
            sums = jnp.dot(helped[0, mine, :], lent[j, :deep_helped, :], preferred_element_type=jnp.float32)
            for c in range(1, HELPED):
                deep = slice(c * deep_helped, (c + 1) * deep_helped)
                sums += jnp.dot(helped[c, mine, :], lent[j, deep, :], preferred_element_type=jnp.float32)
            part[j, 0, k] = sums[:half]
            part[j, 1, k] = sums[half:]
            return 0

        lax.fori_loop(0, 4, column, 0)
        exchange(j).start()

    def join(j):
        exchange(j).wait()
        part[j, core] += inbox[j]

    def take(j):
        mine = pl.ds(pl.multiple_of(core * half, half), half)
        total[:, mine, pl.ds(pl.multiple_of(j * 128, 128), 128)] += inbox[j]

    def hand_over(column):
        return pltpu.make_async_remote_copy(
            src_ref=total.at[column, pl.ds(pl.multiple_of((1 - core) * half, half), half), :],
            dst_ref=other.at[column],
            send_sem=col_send.at[column],
            recv_sem=col_recv.at[column],
            device_id=(me, 1 - core),
            device_id_type=MESH,
        )

    def finish(column):
        hand_over(column).wait()
        mine = total[column, pl.ds(pl.multiple_of(core * half, half), half), :] + other[column]
        for k in range(2):
            start = pl.multiple_of((k * 4 + column) * rows, rows)
            out_ref[pl.ds(start, rows), :] = mine[k * rows : (k + 1) * rows].astype(out_ref.dtype)

    def which(r, blocks):
        found = BLOCKS
        for j, s in enumerate(blocks):
            found = jnp.where(r == s, j, found)
        return found

    def step(r, _):
        incoming(r)

        joined = which(r - SUM_LAG, mid_blocks)

        @pl.when(jnp.logical_and(mid, joined < BLOCKS))
        def _():
            join(joined)

        @pl.when(r < SENDS)
        def _():
            outgoing(lambda copy: copy.start(), r)

        @pl.when(r >= SENT_LAG)
        def _():
            outgoing(lambda copy: copy.wait_send(), r - SENT_LAG)

        @pl.when(r == 1)
        def _():
            total[...] = jnp.zeros_like(total)

        @pl.when(r == 2)
        def _():
            load_amps[1].start()

            @pl.when(mid)
            def _():
                load_amps[0].start()

        @pl.when(r == AMPS_THERE)
        def _():
            load_amps[1].wait()

            @pl.when(mid)
            def _():
                load_amps[0].wait()

        lending = which(r, mid_blocks)

        @pl.when(jnp.logical_and(mid, lending < BLOCKS))
        def _():
            lend(lending)

        def unit(u, _):
            product(pick(mid, u, [code for _, code in mid_at], [code for _, code in end_at]))
            return 0

        before = jnp.where(r > 0, units(r - 1), 0)
        lax.fori_loop(before, units(r), unit, 0)

        taken = which(r, end_blocks)

        @pl.when(jnp.logical_and(end, taken < BLOCKS))
        def _():
            take(taken)

        for q in range(4):

            @pl.when(r == jnp.where(mid, mid_whole[q], end_whole[q]))
            def _():
                hand_over(turned(q)).start()

        return 0

    lax.fori_loop(0, ROUNDS, step, 0)

    def drain(r, _):
        outgoing(lambda copy: copy.wait_send(), r)
        return 0

    lax.fori_loop(ROUNDS - SENT_LAG, SENDS, drain, 0)
    orders = [sorted(range(4), key=lambda q: whole[q]) for whole in (mid_whole, end_whole)]
    for of_mid, of_end in zip(*orders):
        finish(turned(jnp.where(mid, of_mid, of_end)))


def linked(tamps, integrals):
    rows, depth = integrals.shape
    columns = tamps.shape[1]
    return pl.pallas_call(
        kernel,
        out_shape=pltpu.VMEM((8 * rows, columns), jnp.bfloat16),
        in_specs=[pl.BlockSpec(memory_space=pl.ANY)] * 2,
        out_specs=pl.BlockSpec(memory_space=pltpu.VMEM),
        scratch_shapes=[
            pltpu.VMEM((HELPED, 16 * rows, HELPED_WIDE * 128), jnp.bfloat16),
            pltpu.VMEM((PLAIN, 16 * rows, PLAIN_WIDE * 128), jnp.bfloat16),
            pltpu.VMEM((depth, columns), jnp.bfloat16),
            pltpu.VMEM((BLOCKS, HELPED * HELPED_WIDE * 128, 128), jnp.bfloat16),
            pltpu.VMEM((4, 4 * rows, columns), jnp.float32),
            pltpu.VMEM((4, 2 * rows, columns), jnp.float32),
            pltpu.VMEM((BLOCKS, 2, 4, 2 * rows, 128), jnp.float32),
            pltpu.VMEM((BLOCKS, 4, 2 * rows, 128), jnp.float32),
            pltpu.SemaphoreType.DMA((4, SENDS)),
            pltpu.SemaphoreType.DMA((SUMS + 2 * BLOCKS,)),
            pltpu.SemaphoreType.DMA((CHUNKS,)),
            pltpu.SemaphoreType.DMA((2,)),
            pltpu.SemaphoreType.DMA((4,)),
            pltpu.SemaphoreType.DMA((4,)),
            pltpu.SemaphoreType.DMA((BLOCKS,)),
            pltpu.SemaphoreType.DMA((BLOCKS,)),
        ],
        compiler_params=pltpu.CompilerParams(
            collective_id=0, has_side_effects=True, vmem_limit_bytes=56 * 2**20
        ),
    )(tamps, integrals)


def shards(tamps, integrals):
    gathered = lax.all_gather(integrals, "con", axis=0, tiled=True)
    partial_value = jnp.dot(gathered, tamps, preferred_element_type=jnp.float32)
    summed = lax.psum_scatter(partial_value, "rep", scatter_dimension=0, tiled=True)
    return summed.astype(jnp.bfloat16)


def solution(mesh):
    in_specs = (P("rep", "con"), P("con", "rep"))
    out_specs = P("rep", "con")
    part = linked if (mesh.shape["con"], mesh.shape["rep"]) == (16, 2) else shards
    return jax.shard_map(part, mesh=mesh, in_specs=in_specs, out_specs=out_specs, check_vma=False)
```

```python
import functools

import jax
import jax.numpy as jnp
from jax import lax
from jax.experimental import pallas as pl
from jax.experimental.pallas import tpu as pltpu
from jax.sharding import PartitionSpec as P

MESH = pl.DeviceIdType.MESH

HELPED, PLAIN = 2, 5
HELPED_WIDE, PLAIN_WIDE = 7, 10
CHUNKS = HELPED + PLAIN
PER_BLOCK = 4
BLOCKS = 7
SENT_LAG = 5
AMPS_THERE = 5
FIRST = 3
RING = 8
ROUND_US = 2.11
UNIT_US = 0.85
LEND_US = 1.1
SUM_LAG = 1
PIECES = 16 * CHUNKS
WAYS = 4
AMPS = PIECES
SUMS = AMPS + BLOCKS * PER_BLOCK

END_X = (
    2, 3, 6, -1, 62, 11, -1, 61, 67, -1, 59, 20, 4, -1, 19, 66, -1, 41, 75, -1, 102, 97, 107, -1,
    27, 46, -1, 51, 72, -1, 88, 111, 17, -1, 108, 9, -1, 73, 109, -1, 53,
)
END_Y = (
    2, 6, 5, -1, 11, 30, -1, 3, 10, -1, 89, 40, 12, -1, 19, 26, -1, 41, 48, -1, 102, 32, 107, -1,
    16, 94, -1, 55, 20, -1, 52, 54, 100, -1, 17, -1, 109, 80, -1, 37,
)
END_IN = (
    1, 0, 6, 5, 112, 113, 114, 115, 116, 117, 86, -1, 59, 118, 119, 120, 121, 122, 123, 124, 125,
    126, 127, 128, 88, -1, 129, 130, 131, 132, 133, 134, 135, 136, 137, 138, 139, 73, 80, -1, 110,
)
MID_X = (
    12, 8, 7, 13, 15, 11, -1, 5, 71, 21, 22, 56, 57, 42, 98, 78, 59, -1, 107, 102, -1, 104, 46, 62,
    -1, 27, 72, -1, 20, 88, -1, 10, 75, 31, -1, 109, 95, -1, 94, 32,
)
MID_Y = (
    9, 8, 7, 1, 36, 15, 35, 72, 0, 39, -1, 42, 49, 41, 84, 27, -1, 102, 86, -1, 87, 79, 107, -1, 19,
    58, -1, 90, 88, -1, 100, 52, 26, -1, 38, 103, -1, 45, 81, -1, 33,
)
MID_OUT = (
    11, 9, 10, -1, 20, 40, -1, 12, 65, -1, 26, 19, 41, -1, 54, 27, -1, 102, 107, -1, 16, 140, 141,
    142, 143, -1, 144, 52, 17, -1, 145, 146, 147, 109, 148, -1, 149, 150, 151, -1, 152, 153,
)
MID_IN = (
    13, 8, 12, 65, -1, 0, 5, 1, 35, 57, 33, -1, 6, 95, -1, 86, 50, 56, 97, 83, -1, 79, 10, -1, 31,
    76, -1, 90, 75, 88, -1, 100, 32, -1, 38, 44, -1, 82, 3, 103,
)
END_FROM_X = (
    -1, -1, -1, 30, 31, -1, 34, 90, -1, 39, 89, -1, 95, 87, 48, -1, 32, 47, -1, 94, 13, -1, 103, 74,
    69, -1, 79, 55, -1, 18, 23, -1, 100, 60, 83, -1, 45, 80, -1, 37, 101, -1, 81, 25,
)
END_FROM_Y = (
    -1, -1, -1, 58, 62, -1, 61, 67, -1, 86, 59, -1, 66, 33, 96, -1, 68, 75, -1, 82, 97, -1, 104, 46,
    88, -1, 51, 72, -1, 38, 111, -1, 76, 108, 110, -1, 44, 73, -1, 53, 24, -1, 93,
)
END_FROM_MID = (
    -1, -1, -1, 11, 9, -1, 10, 20, -1, 40, 12, -1, 65, 26, 19, -1, 41, 54, -1, 27, 102, -1, 107, 16,
    140, 141, 142, -1, 143, 144, 52, -1, 17, 145, 146, 147, 109, -1, 148, 149, 150, 151, -1, 152,
    153,
)
MID_FROM_X = (
    -1, -1, -1, 40, 36, 35, 41, 43, -1, 39, 33, 99, 49, 50, 84, 85, 14, 70, 106, -1, 87, 79, -1, 74,
    76, 18, -1, 90, 55, -1, 100, 48, -1, 60, 38, 103, -1, 3, 81, -1, 67, 66, -1, 4,
)
MID_FROM_Y = (
    -1, -1, -1, 65, 64, 63, 57, 92, 71, 91, 16, 56, -1, 95, 98, 105, 97, 28, -1, 83, 46, -1, 30, 31,
    23, -1, 51, 75, -1, 2, 34, -1, 32, 44, 108, -1, 82, 94, -1, 47, 101, -1, 25, 89,
)
MID_FROM_MID = (
    -1, -1, -1, 20, 15, 19, -1, 72, 21, 26, 22, 42, 78, -1, 54, 27, -1, 102, 107, 29, 77, 104, -1,
    62, 58, -1, 17, 52, -1, 69, 111, 68, -1, 109, 93, -1, 53, 45, -1, 37, 61, 24, -1, 96,
)
MID_FROM_END = (
    -1, -1, -1, 1, 0, 6, 5, 112, 113, 114, 115, 116, 117, -1, 86, 59, 118, 119, 120, 121, 122, 123,
    124, 125, 126, 127, 128, -1, 88, 129, 130, 131, 132, 133, 134, 135, 136, 137, 138, 139, 73, -1,
    80, 110,
)
END = (END_X, END_Y, END_IN, (-1,))
MID = (MID_X, MID_Y, MID_IN, MID_OUT)
END_FROM = (END_FROM_X, END_FROM_Y, END_FROM_MID, (-1,))
MID_FROM = (MID_FROM_X, MID_FROM_Y, MID_FROM_MID, MID_FROM_END)
SENDS = max(map(len, END + MID))
ROUNDS = max(map(len, END_FROM + MID_FROM))
X, Y, IN, OUT = range(4)
NONE = 255


def parts(code):
    return code // CHUNKS // 4, code // CHUNKS % 4, code % CHUNKS


def arrivals(mid):
    there = {(0, 1 if mid else 0, c): 0 for c in range(CHUNKS)}
    amps, sums = {}, {}
    for table in MID_FROM if mid else END_FROM:
        for r, code in enumerate(table):
            if 0 <= code < PIECES:
                there[parts(code)] = r
            elif AMPS <= code < SUMS:
                amps[(code - AMPS) // PER_BLOCK] = r
            elif code >= SUMS:
                sums[(code - SUMS) // 2] = r
    return there, amps, sums


def plan(mid):
    there, amps, sums = arrivals(mid)
    ready = []
    for q in range(4):
        for c in range(0 if mid else HELPED, CHUNKS):
            ready.append((max(there[q, p, c] for p in range(4)), q, c))
    ready.sort()
    helped_there = max(there[q, p, c] for q in range(4) for p in range(4) for c in range(HELPED)) if mid else 0
    blocks = []
    for j in range(BLOCKS):
        if mid:
            blocks.append(max(amps[j], helped_there, blocks[-1] + 1 if j else 0))
        else:
            blocks.append(sums[j])
    at, credit = [], 0.0
    for r in range(AMPS_THERE, ROUNDS):
        credit = min(credit + ROUND_US, ROUND_US) - LEND_US * blocks.count(r) * mid
        while ready and ready[0][0] <= r and (credit > 0 or r == ROUNDS - 1):
            _, q, c = ready.pop(0)
            at.append((r, q * CHUNKS + c))
            credit -= UNIT_US
    whole = [max(r for r, code in at if code // CHUNKS == q) for q in range(4)]
    return at, whole, blocks


def chosen(index, values):
    while len(values) > 1:
        odd = index % 2 == 1
        index = index // 2
        pairs = [values[i : i + 2] for i in range(0, len(values), 2)]
        values = [jnp.where(odd, v[1], v[0]) if len(v) == 2 else v[0] for v in pairs]
    return values[0]


def pick(mid, index, of_mid, of_end):
    size = ROUNDS + -ROUNDS % 3
    words = []
    for table in (of_mid, of_end):
        full = [NONE if v < 0 else v for v in table] + [NONE] * (size - len(table))
        words.append([full[i] + 256 * full[i + 1] + 65536 * full[i + 2] for i in range(0, size, 3)])
    word = chosen(index // 3, [a if a == b else jnp.where(mid, a, b) for a, b in zip(*words)])
    digit = index % 3
    shifted = jnp.where(digit == 0, word, jnp.where(digit == 1, word // 256, word // 65536))
    return shifted % 256


def number(table, r):
    return sum(code >= 0 for code in table[:r]) % RING


def kernel(
    tamps_hbm, slab_hbm, out_ref, helped, plain, amps, lent, total, other, part, inbox,
    send_sem, recv_sem, own_sem, amps_sem, col_send, col_recv, part_send, part_recv,
):
    me = lax.axis_index("con")
    core = lax.axis_index("rep")
    z, y, x = me // 4, (me // 2) % 2, me % 2
    rows = slab_hbm.shape[0]
    columns = amps.shape[1]
    half = 2 * rows
    own = y * 2 + x
    low = z < 2
    mid = jnp.logical_and(z > 0, z < 3)
    deep_helped, deep_plain = HELPED_WIDE * 128, PLAIN_WIDE * 128
    deep_all_helped = HELPED * deep_helped
    deep_part = deep_all_helped // PER_BLOCK

    def turned(q):
        qx, qy = q % 2, q // 2
        return (y + qy - 2 * y * qy) * 2 + (x + qx - 2 * x * qx)

    neighbour = (
        z * 4 + y * 2 + 1 - x,
        z * 4 + (1 - y) * 2 + x,
        jnp.where(low, me + 4, me - 4),
        jnp.where(low, me - 4, me + 4),
    )
    up, down = jnp.where(low, 2, 3), jnp.where(low, 3, 2)
    sent_by, come_by = (0, 1, up, down), (0, 1, down, up)

    load_amps = [
        pltpu.make_async_copy(
            tamps_hbm.at[pl.ds(first, count), :], amps.at[pl.ds(first, count), :], amps_sem.at[k]
        )
        for k, (first, count) in enumerate(
            ((0, deep_all_helped), (deep_all_helped, PLAIN * deep_plain))
        )
    ]

    def load(c):
        here = pl.ds(pl.multiple_of((own * 4 + z) * rows, rows), rows)
        if c < HELPED:
            cut = slice(c * deep_helped, (c + 1) * deep_helped)
            return pltpu.make_async_copy(slab_hbm.at[:, cut], helped.at[c, here, :], own_sem.at[c])
        first = deep_all_helped + (c - HELPED) * deep_plain
        cut = slice(first, first + deep_plain)
        return pltpu.make_async_copy(slab_hbm.at[:, cut], plain.at[c - HELPED, here, :], own_sem.at[c])

    barrier = pltpu.get_barrier_semaphore()
    for way in (X, Y, IN):
        pl.semaphore_signal(barrier, inc=1, device_id=(neighbour[way], core), device_id_type=MESH)
    pl.semaphore_signal(barrier, inc=1, device_id=(me, 1 - core), device_id_type=MESH)

    @pl.when(mid)
    def _():
        pl.semaphore_signal(barrier, inc=1, device_id=(neighbour[OUT], core), device_id_type=MESH)

    for c in range(CHUNKS):
        load(c).start()
    def coded(table):
        out = []
        for code in table:
            if code < 0:
                out.append(NONE)
            elif code >= SUMS:
                out.append(160 + code - SUMS)
            elif code >= AMPS:
                out.append(128 + code - AMPS)
            else:
                q, p, c = parts(code)
                out.append((q * 4 + p) * 8 + c)
        return out

    def either(of_mid, of_end):
        if isinstance(of_mid, int) and isinstance(of_end, int) and of_mid == of_end:
            return of_mid
        return jnp.where(mid, of_mid, of_end)

    def remote(src, dst, way, lane, index):
        return pltpu.make_async_remote_copy(
            src_ref=src,
            dst_ref=dst,
            send_sem=send_sem.at[way, index],
            recv_sem=recv_sem.at[lane, index],
            device_id=(neighbour[way], core),
            device_id_type=MESH,
        )

    def message(act, code, index, way, lane, amps_too, sums_too):
        q, p, c = code // 32, code // 8 % 4, code % 8
        place = turned(q) * 4 + jnp.where(low, p, 3 - p)
        mine = pl.ds(pl.multiple_of(place * rows, rows), rows)

        @pl.when(jnp.logical_and(code < 128, c < HELPED))
        def _():
            piece = helped.at[c, mine, :]
            act(remote(piece, piece, way, lane, index))

        @pl.when(jnp.logical_and(code < 128, c >= HELPED))
        def _():
            piece = plain.at[c - HELPED, mine, :]
            act(remote(piece, piece, way, lane, index))

        if amps_too:

            @pl.when(jnp.logical_and(code >= 128, code < 160))
            def _():
                k = code - 128
                j = k // PER_BLOCK
                deep = pl.ds(pl.multiple_of(k % PER_BLOCK * deep_part, deep_part), deep_part)
                cut = pl.ds(pl.multiple_of(j * 128, 128), 128)
                act(remote(tamps_hbm.at[deep, cut], lent.at[j, deep, :], way, lane, index))

        if sums_too:

            @pl.when(jnp.logical_and(code >= 160, code < NONE))
            def _():
                k = code - 160
                two = pl.ds(k % 2 * 2, 2)
                act(remote(part.at[k // 2, core, two], inbox.at[k // 2, two], way, lane, index))

    def wait_recv(copy):
        copy.wait_recv()

    def sent(act, code, index, way):
        message(act, code, index, way, sent_by[way], way == IN, way == OUT)

    def start(copy):
        copy.start()

    def wait_send(copy):
        copy.wait_send()

    def counted(n, code):
        return (n + jnp.where(code < NONE, 1, 0)) % RING

    mid_at, mid_whole, mid_blocks = plan(True)
    end_at, end_whole, end_blocks = plan(False)
    assert all(MID_OUT.index(SUMS + 2 * j) >= r + SUM_LAG for j, r in enumerate(mid_blocks))
    assert len(set(end_blocks)) == BLOCKS

    def count_of(at):
        return [sum(s <= r for s, _ in at) for r in range(ROUNDS)]

    def units(r):
        return pick(mid, r, count_of(mid_at), count_of(end_at))

    def which(r, blocks, here):
        found = BLOCKS
        for j, s in enumerate(blocks):
            found = jnp.where(r == s, j, found)
        return jnp.where(here, found, BLOCKS)

    def multiply(left, column, first, deep):
        for start in range(0, columns, 256):
            cut = slice(start, min(start + 256, columns))
            total[column, :, cut] += jnp.dot(
                left, amps[pl.ds(first, deep), cut], preferred_element_type=jnp.float32
            )

    def product(code):
        column, c = turned(code // 8), code % 8
        mine = pl.ds(pl.multiple_of(column * 4 * rows, 4 * rows), 4 * rows)

        @pl.when(c < HELPED)
        def _():
            first = pl.multiple_of(c * deep_helped, 128)
            multiply(helped[c, mine, :], column, first, deep_helped)

        @pl.when(c >= HELPED)
        def _():
            first = pl.multiple_of(deep_all_helped + (c - HELPED) * deep_plain, 128)
            multiply(plain[c - HELPED, mine, :], column, first, deep_plain)

    def exchange(j):
        return pltpu.make_async_remote_copy(
            src_ref=part.at[j, 1 - core],
            dst_ref=inbox.at[j],
            send_sem=part_send.at[j % 2],
            recv_sem=part_recv.at[j % 2],
            device_id=(me, 1 - core),
            device_id_type=MESH,
        )

    def lend(j):
        sums = jnp.dot(helped[0], lent[j, :deep_helped, :], preferred_element_type=jnp.float32)
        for c in range(1, HELPED):
            deep = slice(c * deep_helped, (c + 1) * deep_helped)
            sums += jnp.dot(helped[c], lent[j, deep, :], preferred_element_type=jnp.float32)
        for k in range(4):
            for h in range(2):
                first = (2 * k + h) * half
                part[j, h, k] = sums[first : first + half]
        exchange(j).start()

    def join(j):
        exchange(j).wait()
        part[j, core] += inbox[j]

    def take(j):
        mine = pl.ds(pl.multiple_of(core * half, half), half)
        total[:, mine, pl.ds(pl.multiple_of(j * 128, 128), 128)] += inbox[j]

    def hand_over(column):
        return pltpu.make_async_remote_copy(
            src_ref=total.at[column, pl.ds(pl.multiple_of((1 - core) * half, half), half), :],
            dst_ref=other.at[column],
            send_sem=col_send.at[column],
            recv_sem=col_recv.at[column],
            device_id=(me, 1 - core),
            device_id_type=MESH,
        )

    def finish(column):
        hand_over(column).wait()
        mine = total[column, pl.ds(pl.multiple_of(core * half, half), half), :] + other[column]
        for k in range(2):
            start = pl.multiple_of((k * 4 + column) * rows, rows)
            out_ref[pl.ds(start, rows), :] = mine[k * rows : (k + 1) * rows].astype(out_ref.dtype)

    pl.semaphore_wait(barrier, jnp.where(mid, 5, 4))
    for c in range(CHUNKS):
        load(c).wait()

    ways_out = [(coded(MID[way]), coded(END[way])) for way in range(WAYS)]
    ways_in = [(coded(MID_FROM[way]), coded(END_FROM[way])) for way in range(WAYS)]

    def said_by(r, way):
        code = either(*(table[r] if r < len(table) else NONE for table in ways_out[way]))
        return code, either(number(MID[way], r), number(END[way], r))

    for r in range(FIRST):
        for way in range(WAYS):
            sent(start, *said_by(r, way), way)
    load_amps[1].start()

    @pl.when(mid)
    def _():
        load_amps[0].start()

    total[...] = jnp.zeros_like(total)

    def step(r, carry):
        n_in, n_out, history = carry
        after_in, after_out, now = [], [], []
        for way in range(WAYS):
            code = pick(mid, r, *ways_in[way])
            message(wait_recv, code, n_in[way], way, come_by[way], way == OUT, way == IN)
            after_in.append(counted(n_in[way], code))

        joined = which(r - SUM_LAG, mid_blocks, mid)

        @pl.when(joined < BLOCKS)
        def _():
            join(joined)

        for way in range(WAYS):
            code = pick(mid, r, *ways_out[way])
            sent(start, code, n_out[way], way)
            now.append((code, n_out[way]))
            after_out.append(counted(n_out[way], code))
        for way in range(WAYS):
            sent(wait_send, *history[0][way], way)

        @pl.when(r == AMPS_THERE)
        def _():
            load_amps[1].wait()

            @pl.when(mid)
            def _():
                load_amps[0].wait()

        lending = which(r, mid_blocks, mid)

        @pl.when(lending < BLOCKS)
        def _():
            lend(lending)

        def unit(u, _):
            product(pick(mid, u, *([code // CHUNKS * 8 + code % CHUNKS for _, code in at] for at in (mid_at, end_at))))
            return 0

        lax.fori_loop(units(r - 1), units(r), unit, 0)

        taken = which(r, end_blocks, jnp.logical_not(mid))

        @pl.when(taken < BLOCKS)
        def _():
            take(taken)

        for q in range(4):

            @pl.when(r == jnp.where(mid, mid_whole[q], end_whole[q]))
            def _():
                hand_over(turned(q)).start()

        return after_in, after_out, (*history[1:], now)

    nothing = (jnp.int32(NONE), jnp.int32(0))
    counts = [either(number(MID[way], FIRST), number(END[way], FIRST)) for way in range(WAYS)]
    history = [[nothing] * WAYS] * (SENT_LAG - FIRST)
    history += [[said_by(r, way) for way in range(WAYS)] for r in range(FIRST)]
    first = jax.tree.map(jnp.int32, ([0] * WAYS, counts, tuple(history)))
    lax.fori_loop(FIRST, ROUNDS, step, first)
    for r in range(ROUNDS - SENT_LAG, SENDS):
        for way in range(WAYS):
            if any(r < len(table) and table[r] < NONE for table in ways_out[way]):
                sent(wait_send, *said_by(r, way), way)
    orders = [sorted(range(4), key=lambda q: whole[q]) for whole in (mid_whole, end_whole)]
    for of_mid, of_end in zip(*orders):
        finish(turned(jnp.where(mid, of_mid, of_end)))


def linked(tamps, integrals):
    rows, depth = integrals.shape
    columns = tamps.shape[1]
    return pl.pallas_call(
        kernel,
        out_shape=pltpu.VMEM((8 * rows, columns), jnp.bfloat16),
        in_specs=[pl.BlockSpec(memory_space=pl.ANY)] * 2,
        out_specs=pl.BlockSpec(memory_space=pltpu.VMEM),
        scratch_shapes=[
            pltpu.VMEM((HELPED, 16 * rows, HELPED_WIDE * 128), jnp.bfloat16),
            pltpu.VMEM((PLAIN, 16 * rows, PLAIN_WIDE * 128), jnp.bfloat16),
            pltpu.VMEM((depth, columns), jnp.bfloat16),
            pltpu.VMEM((BLOCKS, HELPED * HELPED_WIDE * 128, 128), jnp.bfloat16),
            pltpu.VMEM((4, 4 * rows, columns), jnp.float32),
            pltpu.VMEM((4, 2 * rows, columns), jnp.float32),
            pltpu.VMEM((BLOCKS, 2, 4, 2 * rows, 128), jnp.float32),
            pltpu.VMEM((BLOCKS, 4, 2 * rows, 128), jnp.float32),
            pltpu.SemaphoreType.DMA((4, RING)),
            pltpu.SemaphoreType.DMA((4, RING)),
            pltpu.SemaphoreType.DMA((CHUNKS,)),
            pltpu.SemaphoreType.DMA((2,)),
            pltpu.SemaphoreType.DMA((4,)),
            pltpu.SemaphoreType.DMA((4,)),
            pltpu.SemaphoreType.DMA((2,)),
            pltpu.SemaphoreType.DMA((2,)),
        ],
        compiler_params=pltpu.CompilerParams(
            collective_id=0, has_side_effects=True, vmem_limit_bytes=56 * 2**20
        ),
    )(tamps, integrals)


def shards(tamps, integrals):
    gathered = lax.all_gather(integrals, "con", axis=0, tiled=True)
    partial_value = jnp.dot(gathered, tamps, preferred_element_type=jnp.float32)
    summed = lax.psum_scatter(partial_value, "rep", scatter_dimension=0, tiled=True)
    return summed.astype(jnp.bfloat16)


def solution(mesh):
    in_specs = (P("rep", "con"), P("con", "rep"))
    out_specs = P("rep", "con")
    part = linked if (mesh.shape["con"], mesh.shape["rep"]) == (16, 2) else shards
    return jax.shard_map(part, mesh=mesh, in_specs=in_specs, out_specs=out_specs, check_vma=False)
```

```python
import functools

import jax
import jax.numpy as jnp
from jax import lax
from jax.experimental import pallas as pl
from jax.experimental.pallas import tpu as pltpu
from jax.sharding import PartitionSpec as P

MESH = pl.DeviceIdType.MESH

HELPED, PLAIN = 2, 5
HELPED_WIDE, PLAIN_WIDE = 7, 10
CHUNKS = HELPED + PLAIN
PER_BLOCK = 4
BLOCKS = 7
SENT_LAG = 5
AMPS_THERE = 5
FIRST = 3
RING = 8
ROUND_US = 2.11
UNIT_US = 0.85
LEND_US = 1.1
SUM_LAG = 1
PIECES = 16 * CHUNKS
WAYS = 4
AMPS = PIECES
SUMS = AMPS + BLOCKS * PER_BLOCK

END_X = (
    2, 3, 6, -1, 62, 11, -1, 61, 67, -1, 59, 20, 4, -1, 19, 66, -1, 41, 75, -1, 102, 97, 107, -1,
    27, 46, -1, 51, 72, -1, 88, 111, 17, -1, 108, 9, -1, 73, 109, -1, 53,
)
END_Y = (
    2, 6, 5, -1, 11, 30, -1, 3, 10, -1, 89, 40, 12, -1, 19, 26, -1, 41, 48, -1, 102, 32, 107, -1,
    16, 94, -1, 55, 20, -1, 52, 54, 100, -1, 17, -1, 109, 80, -1, 37,
)
END_IN = (
    1, 0, 6, 5, 112, 113, 114, 115, 116, 117, 86, -1, 59, 118, 119, 120, 121, 122, 123, 124, 125,
    126, 127, 128, 88, -1, 129, 130, 131, 132, 133, 134, 135, 136, 137, 138, 139, 73, 80, -1, 110,
)
MID_X = (
    12, 8, 7, 13, 15, 11, -1, 5, 71, 21, 22, 56, 57, 42, 98, 78, 59, -1, 107, 102, -1, 104, 46, 62,
    -1, 27, 72, -1, 20, 88, -1, 10, 75, 31, -1, 109, 95, -1, 94, 32,
)
MID_Y = (
    9, 8, 7, 1, 36, 15, 35, 72, 0, 39, -1, 42, 49, 41, 84, 27, -1, 102, 86, -1, 87, 79, 107, -1, 19,
    58, -1, 90, 88, -1, 100, 52, 26, -1, 38, 103, -1, 45, 81, -1, 33,
)
MID_OUT = (
    11, 9, 10, -1, 20, 40, -1, 12, 65, -1, 26, 19, 41, -1, 54, 27, -1, 102, 107, -1, 16, 140, 141,
    142, 143, -1, 144, 52, 17, -1, 145, 146, 147, 109, 148, -1, 149, 150, 151, -1, 152, 153,
)
MID_IN = (
    13, 8, 12, 65, -1, 0, 5, 1, 35, 57, 33, -1, 6, 95, -1, 86, 50, 56, 97, 83, -1, 79, 10, -1, 31,
    76, -1, 90, 75, 88, -1, 100, 32, -1, 38, 44, -1, 82, 3, 103,
)
END_FROM_X = (
    -1, -1, -1, 30, 31, -1, 34, 90, -1, 39, 89, -1, 95, 87, 48, -1, 32, 47, -1, 94, 13, -1, 103, 74,
    69, -1, 79, 55, -1, 18, 23, -1, 100, 60, 83, -1, 45, 80, -1, 37, 101, -1, 81, 25,
)
END_FROM_Y = (
    -1, -1, -1, 58, 62, -1, 61, 67, -1, 86, 59, -1, 66, 33, 96, -1, 68, 75, -1, 82, 97, -1, 104, 46,
    88, -1, 51, 72, -1, 38, 111, -1, 76, 108, 110, -1, 44, 73, -1, 53, 24, -1, 93,
)
END_FROM_MID = (
    -1, -1, -1, 11, 9, -1, 10, 20, -1, 40, 12, -1, 65, 26, 19, -1, 41, 54, -1, 27, 102, -1, 107, 16,
    140, 141, 142, -1, 143, 144, 52, -1, 17, 145, 146, 147, 109, -1, 148, 149, 150, 151, -1, 152,
    153,
)
MID_FROM_X = (
    -1, -1, -1, 40, 36, 35, 41, 43, -1, 39, 33, 99, 49, 50, 84, 85, 14, 70, 106, -1, 87, 79, -1, 74,
    76, 18, -1, 90, 55, -1, 100, 48, -1, 60, 38, 103, -1, 3, 81, -1, 67, 66, -1, 4,
)
MID_FROM_Y = (
    -1, -1, -1, 65, 64, 63, 57, 92, 71, 91, 16, 56, -1, 95, 98, 105, 97, 28, -1, 83, 46, -1, 30, 31,
    23, -1, 51, 75, -1, 2, 34, -1, 32, 44, 108, -1, 82, 94, -1, 47, 101, -1, 25, 89,
)
MID_FROM_MID = (
    -1, -1, -1, 20, 15, 19, -1, 72, 21, 26, 22, 42, 78, -1, 54, 27, -1, 102, 107, 29, 77, 104, -1,
    62, 58, -1, 17, 52, -1, 69, 111, 68, -1, 109, 93, -1, 53, 45, -1, 37, 61, 24, -1, 96,
)
MID_FROM_END = (
    -1, -1, -1, 1, 0, 6, 5, 112, 113, 114, 115, 116, 117, -1, 86, 59, 118, 119, 120, 121, 122, 123,
    124, 125, 126, 127, 128, -1, 88, 129, 130, 131, 132, 133, 134, 135, 136, 137, 138, 139, 73, -1,
    80, 110,
)
END = (END_X, END_Y, END_IN, (-1,))
MID = (MID_X, MID_Y, MID_IN, MID_OUT)
END_FROM = (END_FROM_X, END_FROM_Y, END_FROM_MID, (-1,))
MID_FROM = (MID_FROM_X, MID_FROM_Y, MID_FROM_MID, MID_FROM_END)
SENDS = max(map(len, END + MID))
ROUNDS = max(map(len, END_FROM + MID_FROM))
X, Y, IN, OUT = range(4)
NONE = 255


def parts(code):
    return code // CHUNKS // 4, code // CHUNKS % 4, code % CHUNKS


def arrivals(mid):
    there = {(0, 1 if mid else 0, c): 0 for c in range(CHUNKS)}
    amps, sums = {}, {}
    for table in MID_FROM if mid else END_FROM:
        for r, code in enumerate(table):
            if 0 <= code < PIECES:
                there[parts(code)] = r
            elif AMPS <= code < SUMS:
                amps[(code - AMPS) // PER_BLOCK] = r
            elif code >= SUMS:
                sums[(code - SUMS) // 2] = r
    return there, amps, sums


def plan(mid):
    there, amps, sums = arrivals(mid)
    ready = []
    for q in range(4):
        for c in range(0 if mid else HELPED, CHUNKS):
            ready.append((max(there[q, p, c] for p in range(4)), q, c))
    ready.sort()
    helped_there = max(there[q, p, c] for q in range(4) for p in range(4) for c in range(HELPED)) if mid else 0
    blocks = []
    for j in range(BLOCKS):
        if mid:
            blocks.append(max(amps[j], helped_there, blocks[-1] + 1 if j else 0))
        else:
            blocks.append(sums[j])
    at, credit = [], 0.0
    for r in range(AMPS_THERE, ROUNDS):
        credit = min(credit + ROUND_US, ROUND_US) - LEND_US * blocks.count(r) * mid
        while ready and ready[0][0] <= r and (credit > 0 or r == ROUNDS - 1):
            _, q, c = ready.pop(0)
            at.append((r, q * CHUNKS + c))
            credit -= UNIT_US
    whole = [max(u for u, (_, code) in enumerate(at) if code // CHUNKS == q) for q in range(4)]
    return at, whole, blocks


def chosen(index, values):
    while len(values) > 1:
        odd = index % 2 == 1
        index = index // 2
        pairs = [values[i : i + 2] for i in range(0, len(values), 2)]
        values = [jnp.where(odd, v[1], v[0]) if len(v) == 2 else v[0] for v in pairs]
    return values[0]


def pick(mid, index, of_mid, of_end):
    size = ROUNDS + -ROUNDS % 3
    words = []
    for table in (of_mid, of_end):
        full = [NONE if v < 0 else v for v in table] + [NONE] * (size - len(table))
        words.append([full[i] + 256 * full[i + 1] + 65536 * full[i + 2] for i in range(0, size, 3)])
    word = chosen(index // 3, [a if a == b else jnp.where(mid, a, b) for a, b in zip(*words)])
    digit = index % 3
    shifted = jnp.where(digit == 0, word, jnp.where(digit == 1, word // 256, word // 65536))
    return shifted % 256


def number(table, r):
    return sum(code >= 0 for code in table[:r]) % RING


def kernel(
    tamps_hbm, slab_hbm, out_ref, helped, plain, amps, lent, total, other, part, inbox,
    send_sem, recv_sem, own_sem, amps_sem, col_send, col_recv, part_send, part_recv,
):
    me = lax.axis_index("con")
    core = lax.axis_index("rep")
    z, y, x = me // 4, (me // 2) % 2, me % 2
    rows = slab_hbm.shape[0]
    columns = amps.shape[1]
    half = 2 * rows
    own = y * 2 + x
    low = z < 2
    mid = jnp.logical_and(z > 0, z < 3)
    deep_helped, deep_plain = HELPED_WIDE * 128, PLAIN_WIDE * 128
    deep_all_helped = HELPED * deep_helped
    deep_part = deep_all_helped // PER_BLOCK

    def turned(q):
        qx, qy = q % 2, q // 2
        return (y + qy - 2 * y * qy) * 2 + (x + qx - 2 * x * qx)

    neighbour = (
        z * 4 + y * 2 + 1 - x,
        z * 4 + (1 - y) * 2 + x,
        jnp.where(low, me + 4, me - 4),
        jnp.where(low, me - 4, me + 4),
    )
    up, down = jnp.where(low, 2, 3), jnp.where(low, 3, 2)
    sent_by, come_by = (0, 1, up, down), (0, 1, down, up)

    load_amps = [
        pltpu.make_async_copy(
            tamps_hbm.at[pl.ds(first, count), :], amps.at[pl.ds(first, count), :], amps_sem.at[k]
        )
        for k, (first, count) in enumerate(
            ((0, deep_all_helped), (deep_all_helped, PLAIN * deep_plain))
        )
    ]

    def load(c):
        here = pl.ds(pl.multiple_of((own * 4 + z) * rows, rows), rows)
        if c < HELPED:
            cut = slice(c * deep_helped, (c + 1) * deep_helped)
            return pltpu.make_async_copy(slab_hbm.at[:, cut], helped.at[c, here, :], own_sem.at[c])
        first = deep_all_helped + (c - HELPED) * deep_plain
        cut = slice(first, first + deep_plain)
        return pltpu.make_async_copy(slab_hbm.at[:, cut], plain.at[c - HELPED, here, :], own_sem.at[c])

    barrier = pltpu.get_barrier_semaphore()
    for way in (X, Y, IN):
        pl.semaphore_signal(barrier, inc=1, device_id=(neighbour[way], core), device_id_type=MESH)
    pl.semaphore_signal(barrier, inc=1, device_id=(me, 1 - core), device_id_type=MESH)

    @pl.when(mid)
    def _():
        pl.semaphore_signal(barrier, inc=1, device_id=(neighbour[OUT], core), device_id_type=MESH)

    for c in range(CHUNKS):
        load(c).start()
    def coded(table):
        out = []
        for code in table:
            if code < 0:
                out.append(NONE)
            elif code >= SUMS:
                out.append(160 + code - SUMS)
            elif code >= AMPS:
                out.append(128 + code - AMPS)
            else:
                q, p, c = parts(code)
                out.append((q * 4 + p) * 8 + c)
        return out

    def either(of_mid, of_end):
        if isinstance(of_mid, int) and isinstance(of_end, int) and of_mid == of_end:
            return of_mid
        return jnp.where(mid, of_mid, of_end)

    def remote(src, dst, way, lane, index):
        return pltpu.make_async_remote_copy(
            src_ref=src,
            dst_ref=dst,
            send_sem=send_sem.at[way, index],
            recv_sem=recv_sem.at[lane, index],
            device_id=(neighbour[way], core),
            device_id_type=MESH,
        )

    def message(act, code, index, way, lane, amps_too, sums_too):
        q, p, c = code // 32, code // 8 % 4, code % 8
        place = turned(q) * 4 + jnp.where(low, p, 3 - p)
        mine = pl.ds(pl.multiple_of(place * rows, rows), rows)

        @pl.when(jnp.logical_and(code < 128, c < HELPED))
        def _():
            piece = helped.at[c, mine, :]
            act(remote(piece, piece, way, lane, index))

        @pl.when(jnp.logical_and(code < 128, c >= HELPED))
        def _():
            piece = plain.at[c - HELPED, mine, :]
            act(remote(piece, piece, way, lane, index))

        if amps_too:

            @pl.when(jnp.logical_and(code >= 128, code < 160))
            def _():
                k = code - 128
                j = k // PER_BLOCK
                deep = pl.ds(pl.multiple_of(k % PER_BLOCK * deep_part, deep_part), deep_part)
                cut = pl.ds(pl.multiple_of(j * 128, 128), 128)
                act(remote(tamps_hbm.at[deep, cut], lent.at[j, deep, :], way, lane, index))

        if sums_too:

            @pl.when(jnp.logical_and(code >= 160, code < NONE))
            def _():
                k = code - 160
                two = pl.ds(k % 2 * 2, 2)
                act(remote(part.at[k // 2, core, two], inbox.at[k // 2, two], way, lane, index))

    def wait_recv(copy):
        copy.wait_recv()

    def sent(act, code, index, way):
        message(act, code, index, way, sent_by[way], way == IN, way == OUT)

    def start(copy):
        copy.start()

    def wait_send(copy):
        copy.wait_send()

    def counted(n, code):
        return (n + jnp.where(code < NONE, 1, 0)) % RING

    mid_at, mid_whole, mid_blocks = plan(True)
    end_at, end_whole, end_blocks = plan(False)
    assert all(MID_OUT.index(SUMS + 2 * j) >= r + SUM_LAG for j, r in enumerate(mid_blocks))
    assert len(set(end_blocks)) == BLOCKS

    def count_of(at):
        return [sum(s <= r for s, _ in at) for r in range(ROUNDS)]

    def units(r):
        return pick(mid, r, count_of(mid_at), count_of(end_at))

    def which(r, blocks, here):
        found = BLOCKS
        for j, s in enumerate(blocks):
            found = jnp.where(r == s, j, found)
        return jnp.where(here, found, BLOCKS)

    def multiply(left, column, first, deep):
        for start in range(0, columns, 256):
            cut = slice(start, min(start + 256, columns))
            total[column, :, cut] += jnp.dot(
                left, amps[pl.ds(first, deep), cut], preferred_element_type=jnp.float32
            )

    def product(code):
        column, c = turned(code // 8), code % 8
        mine = pl.ds(pl.multiple_of(column * 4 * rows, 4 * rows), 4 * rows)

        @pl.when(c < HELPED)
        def _():
            first = pl.multiple_of(c * deep_helped, 128)
            multiply(helped[c, mine, :], column, first, deep_helped)

        @pl.when(c >= HELPED)
        def _():
            first = pl.multiple_of(deep_all_helped + (c - HELPED) * deep_plain, 128)
            multiply(plain[c - HELPED, mine, :], column, first, deep_plain)

    def exchange(j):
        return pltpu.make_async_remote_copy(
            src_ref=part.at[j, 1 - core],
            dst_ref=inbox.at[j],
            send_sem=part_send.at[j % 2],
            recv_sem=part_recv.at[j % 2],
            device_id=(me, 1 - core),
            device_id_type=MESH,
        )

    def lend(j):
        sums = jnp.dot(helped[0], lent[j, :deep_helped, :], preferred_element_type=jnp.float32)
        for c in range(1, HELPED):
            deep = slice(c * deep_helped, (c + 1) * deep_helped)
            sums += jnp.dot(helped[c], lent[j, deep, :], preferred_element_type=jnp.float32)
        for k in range(4):
            for h in range(2):
                first = (2 * k + h) * half
                part[j, h, k] = sums[first : first + half]
        exchange(j).start()

    def join(j):
        exchange(j).wait()
        part[j, core] += inbox[j]

    def take(j):
        mine = pl.ds(pl.multiple_of(core * half, half), half)
        total[:, mine, pl.ds(pl.multiple_of(j * 128, 128), 128)] += inbox[j]

    def hand_over(column):
        return pltpu.make_async_remote_copy(
            src_ref=total.at[column, pl.ds(pl.multiple_of((1 - core) * half, half), half), :],
            dst_ref=other.at[column],
            send_sem=col_send.at[column],
            recv_sem=col_recv.at[column],
            device_id=(me, 1 - core),
            device_id_type=MESH,
        )

    def finish(column):
        hand_over(column).wait()
        mine = total[column, pl.ds(pl.multiple_of(core * half, half), half), :] + other[column]
        for k in range(2):
            start = pl.multiple_of((k * 4 + column) * rows, rows)
            out_ref[pl.ds(start, rows), :] = mine[k * rows : (k + 1) * rows].astype(out_ref.dtype)

    pl.semaphore_wait(barrier, jnp.where(mid, 5, 4))
    for c in range(CHUNKS):
        load(c).wait()

    ways_out = [(coded(MID[way]), coded(END[way])) for way in range(WAYS)]
    ways_in = [(coded(MID_FROM[way]), coded(END_FROM[way])) for way in range(WAYS)]

    def said_by(r, way):
        code = either(*(table[r] if r < len(table) else NONE for table in ways_out[way]))
        return code, either(number(MID[way], r), number(END[way], r))

    for r in range(FIRST):
        for way in range(WAYS):
            sent(start, *said_by(r, way), way)
    load_amps[1].start()

    @pl.when(mid)
    def _():
        load_amps[0].start()

    total[...] = jnp.zeros_like(total)

    def step(r, carry):
        n_in, n_out, history = carry
        after_in, after_out, now = [], [], []
        for way in range(WAYS):
            code = pick(mid, r, *ways_in[way])
            message(wait_recv, code, n_in[way], way, come_by[way], way == OUT, way == IN)
            after_in.append(counted(n_in[way], code))

        joined = which(r - SUM_LAG, mid_blocks, mid)

        @pl.when(joined < BLOCKS)
        def _():
            join(joined)

        for way in range(WAYS):
            code = pick(mid, r, *ways_out[way])
            sent(start, code, n_out[way], way)
            now.append((code, n_out[way]))
            after_out.append(counted(n_out[way], code))
        for way in range(WAYS):
            sent(wait_send, *history[0][way], way)

        @pl.when(r == AMPS_THERE)
        def _():
            load_amps[1].wait()

            @pl.when(mid)
            def _():
                load_amps[0].wait()

        lending = which(r, mid_blocks, mid)

        @pl.when(lending < BLOCKS)
        def _():
            lend(lending)

        def unit(u, _):
            product(pick(mid, u, *([code // CHUNKS * 8 + code % CHUNKS for _, code in at] for at in (mid_at, end_at))))
            for q in range(4):

                @pl.when(u == jnp.where(mid, mid_whole[q], end_whole[q]))
                def _():
                    hand_over(turned(q)).start()

            return 0

        lax.fori_loop(units(r - 1), units(r), unit, 0)

        taken = which(r, end_blocks, jnp.logical_not(mid))

        @pl.when(taken < BLOCKS)
        def _():
            take(taken)

        return after_in, after_out, (*history[1:], now)

    nothing = (jnp.int32(NONE), jnp.int32(0))
    counts = [either(number(MID[way], FIRST), number(END[way], FIRST)) for way in range(WAYS)]
    history = [[nothing] * WAYS] * (SENT_LAG - FIRST)
    history += [[said_by(r, way) for way in range(WAYS)] for r in range(FIRST)]
    first = jax.tree.map(jnp.int32, ([0] * WAYS, counts, tuple(history)))
    lax.fori_loop(FIRST, ROUNDS, step, first)
    for r in range(ROUNDS - SENT_LAG, SENDS):
        for way in range(WAYS):
            if any(r < len(table) and table[r] < NONE for table in ways_out[way]):
                sent(wait_send, *said_by(r, way), way)
    orders = [sorted(range(4), key=lambda q: whole[q]) for whole in (mid_whole, end_whole)]
    for of_mid, of_end in zip(*orders):
        finish(turned(jnp.where(mid, of_mid, of_end)))


def linked(tamps, integrals):
    rows, depth = integrals.shape
    columns = tamps.shape[1]
    return pl.pallas_call(
        kernel,
        out_shape=pltpu.VMEM((8 * rows, columns), jnp.bfloat16),
        in_specs=[pl.BlockSpec(memory_space=pl.ANY)] * 2,
        out_specs=pl.BlockSpec(memory_space=pltpu.VMEM),
        scratch_shapes=[
            pltpu.VMEM((HELPED, 16 * rows, HELPED_WIDE * 128), jnp.bfloat16),
            pltpu.VMEM((PLAIN, 16 * rows, PLAIN_WIDE * 128), jnp.bfloat16),
            pltpu.VMEM((depth, columns), jnp.bfloat16),
            pltpu.VMEM((BLOCKS, HELPED * HELPED_WIDE * 128, 128), jnp.bfloat16),
            pltpu.VMEM((4, 4 * rows, columns), jnp.float32),
            pltpu.VMEM((4, 2 * rows, columns), jnp.float32),
            pltpu.VMEM((BLOCKS, 2, 4, 2 * rows, 128), jnp.float32),
            pltpu.VMEM((BLOCKS, 4, 2 * rows, 128), jnp.float32),
            pltpu.SemaphoreType.DMA((4, RING)),
            pltpu.SemaphoreType.DMA((4, RING)),
            pltpu.SemaphoreType.DMA((CHUNKS,)),
            pltpu.SemaphoreType.DMA((2,)),
            pltpu.SemaphoreType.DMA((4,)),
            pltpu.SemaphoreType.DMA((4,)),
            pltpu.SemaphoreType.DMA((2,)),
            pltpu.SemaphoreType.DMA((2,)),
        ],
        compiler_params=pltpu.CompilerParams(
            collective_id=0, has_side_effects=True, vmem_limit_bytes=56 * 2**20
        ),
    )(tamps, integrals)


def shards(tamps, integrals):
    gathered = lax.all_gather(integrals, "con", axis=0, tiled=True)
    partial_value = jnp.dot(gathered, tamps, preferred_element_type=jnp.float32)
    summed = lax.psum_scatter(partial_value, "rep", scatter_dimension=0, tiled=True)
    return summed.astype(jnp.bfloat16)


def solution(mesh):
    in_specs = (P("rep", "con"), P("con", "rep"))
    out_specs = P("rep", "con")
    part = linked if (mesh.shape["con"], mesh.shape["rep"]) == (16, 2) else shards
    return jax.shard_map(part, mesh=mesh, in_specs=in_specs, out_specs=out_specs, check_vma=False)
```

```python
import functools

import jax
import jax.numpy as jnp
from jax import lax
from jax.experimental import pallas as pl
from jax.experimental.pallas import tpu as pltpu
from jax.sharding import PartitionSpec as P

MESH = pl.DeviceIdType.MESH

HELPED, PLAIN = 2, 5
HELPED_WIDE, PLAIN_WIDE = 7, 10
CHUNKS = HELPED + PLAIN
PER_BLOCK = 4
BLOCKS = 7
SENT_LAG = 4
AMPS_THERE = 5
FIRST = 3
RING = 8
ROUND_US = 3.5
UNIT_US = 0.85
LEND_US = 1.1
SUM_LAG = 1
PIECES = 16 * CHUNKS
WAYS = 4
AMPS = PIECES
SUMS = AMPS + BLOCKS * PER_BLOCK

END_X = (
    2, 3, 6, -1, 62, 11, -1, 61, 67, -1, 59, 20, 4, -1, 19, 66, -1, 41, 75, -1, 102, 97, 107, -1,
    27, 46, -1, 51, 72, -1, 88, 111, 17, -1, 108, 9, -1, 73, 109, -1, 53,
)
END_Y = (
    2, 6, 5, -1, 11, 30, -1, 3, 10, -1, 89, 40, 12, -1, 19, 26, -1, 41, 48, -1, 102, 32, 107, -1,
    16, 94, -1, 55, 20, -1, 52, 54, 100, -1, 17, -1, 109, 80, -1, 37,
)
END_IN = (
    1, 0, 6, 5, 112, 113, 114, 115, 116, 117, 86, -1, 59, 118, 119, 120, 121, 122, 123, 124, 125,
    126, 127, 128, 88, -1, 129, 130, 131, 132, 133, 134, 135, 136, 137, 138, 139, 73, 80, -1, 110,
)
MID_X = (
    12, 8, 7, 13, 15, 11, -1, 5, 71, 21, 22, 56, 57, 42, 98, 78, 59, -1, 107, 102, -1, 104, 46, 62,
    -1, 27, 72, -1, 20, 88, -1, 10, 75, 31, -1, 109, 95, -1, 94, 32,
)
MID_Y = (
    9, 8, 7, 1, 36, 15, 35, 72, 0, 39, -1, 42, 49, 41, 84, 27, -1, 102, 86, -1, 87, 79, 107, -1, 19,
    58, -1, 90, 88, -1, 100, 52, 26, -1, 38, 103, -1, 45, 81, -1, 33,
)
MID_OUT = (
    11, 9, 10, -1, 20, 40, -1, 12, 65, -1, 26, 19, 41, -1, 54, 27, -1, 102, 107, -1, 16, 140, 141,
    142, 143, -1, 144, 52, 17, -1, 145, 146, 147, 109, 148, -1, 149, 150, 151, -1, 152, 153,
)
MID_IN = (
    13, 8, 12, 65, -1, 0, 5, 1, 35, 57, 33, -1, 6, 95, -1, 86, 50, 56, 97, 83, -1, 79, 10, -1, 31,
    76, -1, 90, 75, 88, -1, 100, 32, -1, 38, 44, -1, 82, 3, 103,
)
END_FROM_X = (
    -1, -1, -1, 30, 31, -1, 34, 90, -1, 39, 89, -1, 95, 87, 48, -1, 32, 47, -1, 94, 13, -1, 103, 74,
    69, -1, 79, 55, -1, 18, 23, -1, 100, 60, 83, -1, 45, 80, -1, 37, 101, -1, 81, 25,
)
END_FROM_Y = (
    -1, -1, -1, 58, 62, -1, 61, 67, -1, 86, 59, -1, 66, 33, 96, -1, 68, 75, -1, 82, 97, -1, 104, 46,
    88, -1, 51, 72, -1, 38, 111, -1, 76, 108, 110, -1, 44, 73, -1, 53, 24, -1, 93,
)
END_FROM_MID = (
    -1, -1, -1, 11, 9, -1, 10, 20, -1, 40, 12, -1, 65, 26, 19, -1, 41, 54, -1, 27, 102, -1, 107, 16,
    140, 141, 142, -1, 143, 144, 52, -1, 17, 145, 146, 147, 109, -1, 148, 149, 150, 151, -1, 152,
    153,
)
MID_FROM_X = (
    -1, -1, -1, 40, 36, 35, 41, 43, -1, 39, 33, 99, 49, 50, 84, 85, 14, 70, 106, -1, 87, 79, -1, 74,
    76, 18, -1, 90, 55, -1, 100, 48, -1, 60, 38, 103, -1, 3, 81, -1, 67, 66, -1, 4,
)
MID_FROM_Y = (
    -1, -1, -1, 65, 64, 63, 57, 92, 71, 91, 16, 56, -1, 95, 98, 105, 97, 28, -1, 83, 46, -1, 30, 31,
    23, -1, 51, 75, -1, 2, 34, -1, 32, 44, 108, -1, 82, 94, -1, 47, 101, -1, 25, 89,
)
MID_FROM_MID = (
    -1, -1, -1, 20, 15, 19, -1, 72, 21, 26, 22, 42, 78, -1, 54, 27, -1, 102, 107, 29, 77, 104, -1,
    62, 58, -1, 17, 52, -1, 69, 111, 68, -1, 109, 93, -1, 53, 45, -1, 37, 61, 24, -1, 96,
)
MID_FROM_END = (
    -1, -1, -1, 1, 0, 6, 5, 112, 113, 114, 115, 116, 117, -1, 86, 59, 118, 119, 120, 121, 122, 123,
    124, 125, 126, 127, 128, -1, 88, 129, 130, 131, 132, 133, 134, 135, 136, 137, 138, 139, 73, -1,
    80, 110,
)
END = (END_X, END_Y, END_IN, (-1,))
MID = (MID_X, MID_Y, MID_IN, MID_OUT)
END_FROM = (END_FROM_X, END_FROM_Y, END_FROM_MID, (-1,))
MID_FROM = (MID_FROM_X, MID_FROM_Y, MID_FROM_MID, MID_FROM_END)
SENDS = max(map(len, END + MID))
ROUNDS = max(map(len, END_FROM + MID_FROM))
X, Y, IN, OUT = range(4)
NONE = 255


def parts(code):
    return code // CHUNKS // 4, code // CHUNKS % 4, code % CHUNKS


def arrivals(mid):
    there = {(0, 1 if mid else 0, c): 0 for c in range(CHUNKS)}
    amps, sums = {}, {}
    for table in MID_FROM if mid else END_FROM:
        for r, code in enumerate(table):
            if 0 <= code < PIECES:
                there[parts(code)] = r
            elif AMPS <= code < SUMS:
                amps[(code - AMPS) // PER_BLOCK] = r
            elif code >= SUMS:
                sums[(code - SUMS) // 2] = r
    return there, amps, sums


def plan(mid):
    there, amps, sums = arrivals(mid)
    ready = []
    for q in range(4):
        for c in range(0 if mid else HELPED, CHUNKS):
            ready.append((max(there[q, p, c] for p in range(4)), q, c))
    ready.sort()
    helped_there = max(there[q, p, c] for q in range(4) for p in range(4) for c in range(HELPED)) if mid else 0
    blocks = []
    for j in range(BLOCKS):
        if mid:
            blocks.append(max(amps[j], helped_there, blocks[-1] + 1 if j else 0))
        else:
            blocks.append(sums[j])
    at, credit = [], 0.0
    for r in range(AMPS_THERE, ROUNDS):
        credit = min(credit + ROUND_US, ROUND_US) - LEND_US * blocks.count(r) * mid
        while ready and ready[0][0] <= r and (credit > 0 or r == ROUNDS - 1):
            _, q, c = ready.pop(0)
            at.append((r, q * CHUNKS + c))
            credit -= UNIT_US
    whole = [max(u for u, (_, code) in enumerate(at) if code // CHUNKS == q) for q in range(4)]
    return at, whole, blocks


def chosen(index, values):
    while len(values) > 1:
        odd = index % 2 == 1
        index = index // 2
        pairs = [values[i : i + 2] for i in range(0, len(values), 2)]
        values = [jnp.where(odd, v[1], v[0]) if len(v) == 2 else v[0] for v in pairs]
    return values[0]


def pick(mid, index, of_mid, of_end):
    size = ROUNDS + -ROUNDS % 3
    words = []
    for table in (of_mid, of_end):
        full = [NONE if v < 0 else v for v in table] + [NONE] * (size - len(table))
        words.append([full[i] + 256 * full[i + 1] + 65536 * full[i + 2] for i in range(0, size, 3)])
    word = chosen(index // 3, [a if a == b else jnp.where(mid, a, b) for a, b in zip(*words)])
    digit = index % 3
    shifted = jnp.where(digit == 0, word, jnp.where(digit == 1, word // 256, word // 65536))
    return shifted % 256


def number(table, r):
    return sum(code >= 0 for code in table[:r]) % RING


def kernel(
    tamps_hbm, slab_hbm, out_ref, helped, plain, amps, lent, total, other, part, inbox,
    send_sem, recv_sem, own_sem, amps_sem, col_send, col_recv, part_send, part_recv,
):
    me = lax.axis_index("con")
    core = lax.axis_index("rep")
    z, y, x = me // 4, (me // 2) % 2, me % 2
    rows = slab_hbm.shape[0]
    columns = amps.shape[1]
    half = 2 * rows
    own = y * 2 + x
    low = z < 2
    mid = jnp.logical_and(z > 0, z < 3)
    deep_helped, deep_plain = HELPED_WIDE * 128, PLAIN_WIDE * 128
    deep_all_helped = HELPED * deep_helped
    deep_part = deep_all_helped // PER_BLOCK

    def turned(q):
        qx, qy = q % 2, q // 2
        return (y + qy - 2 * y * qy) * 2 + (x + qx - 2 * x * qx)

    neighbour = (
        z * 4 + y * 2 + 1 - x,
        z * 4 + (1 - y) * 2 + x,
        jnp.where(low, me + 4, me - 4),
        jnp.where(low, me - 4, me + 4),
    )
    up, down = jnp.where(low, 2, 3), jnp.where(low, 3, 2)
    sent_by, come_by = (0, 1, up, down), (0, 1, down, up)

    load_amps = [
        pltpu.make_async_copy(
            tamps_hbm.at[pl.ds(first, count), :], amps.at[pl.ds(first, count), :], amps_sem.at[k]
        )
        for k, (first, count) in enumerate(
            ((0, deep_all_helped), (deep_all_helped, PLAIN * deep_plain))
        )
    ]

    def load(c):
        here = pl.ds(pl.multiple_of((own * 4 + z) * rows, rows), rows)
        if c < HELPED:
            cut = slice(c * deep_helped, (c + 1) * deep_helped)
            return pltpu.make_async_copy(slab_hbm.at[:, cut], helped.at[c, here, :], own_sem.at[c])
        first = deep_all_helped + (c - HELPED) * deep_plain
        cut = slice(first, first + deep_plain)
        return pltpu.make_async_copy(slab_hbm.at[:, cut], plain.at[c - HELPED, here, :], own_sem.at[c])

    barrier = pltpu.get_barrier_semaphore()
    for way in (X, Y, IN):
        pl.semaphore_signal(barrier, inc=1, device_id=(neighbour[way], core), device_id_type=MESH)
    pl.semaphore_signal(barrier, inc=1, device_id=(me, 1 - core), device_id_type=MESH)

    @pl.when(mid)
    def _():
        pl.semaphore_signal(barrier, inc=1, device_id=(neighbour[OUT], core), device_id_type=MESH)

    for c in range(CHUNKS):
        load(c).start()
    def coded(table):
        out = []
        for code in table:
            if code < 0:
                out.append(NONE)
            elif code >= SUMS:
                out.append(160 + code - SUMS)
            elif code >= AMPS:
                out.append(128 + code - AMPS)
            else:
                q, p, c = parts(code)
                out.append((q * 4 + p) * 8 + c)
        return out

    def either(of_mid, of_end):
        if isinstance(of_mid, int) and isinstance(of_end, int) and of_mid == of_end:
            return of_mid
        return jnp.where(mid, of_mid, of_end)

    def remote(src, dst, way, lane, index):
        return pltpu.make_async_remote_copy(
            src_ref=src,
            dst_ref=dst,
            send_sem=send_sem.at[way, index],
            recv_sem=recv_sem.at[lane, index],
            device_id=(neighbour[way], core),
            device_id_type=MESH,
        )

    def message(act, code, index, way, lane, amps_too, sums_too):
        q, p, c = code // 32, code // 8 % 4, code % 8
        place = turned(q) * 4 + jnp.where(low, p, 3 - p)
        mine = pl.ds(pl.multiple_of(place * rows, rows), rows)

        @pl.when(jnp.logical_and(code < 128, c < HELPED))
        def _():
            piece = helped.at[c, mine, :]
            act(remote(piece, piece, way, lane, index))

        @pl.when(jnp.logical_and(code < 128, c >= HELPED))
        def _():
            piece = plain.at[c - HELPED, mine, :]
            act(remote(piece, piece, way, lane, index))

        if amps_too:

            @pl.when(jnp.logical_and(code >= 128, code < 160))
            def _():
                k = code - 128
                j = k // PER_BLOCK
                deep = pl.ds(pl.multiple_of(k % PER_BLOCK * deep_part, deep_part), deep_part)
                cut = pl.ds(pl.multiple_of(j * 128, 128), 128)
                act(remote(tamps_hbm.at[deep, cut], lent.at[j, deep, :], way, lane, index))

        if sums_too:

            @pl.when(jnp.logical_and(code >= 160, code < NONE))
            def _():
                k = code - 160
                two = pl.ds(k % 2 * 2, 2)
                act(remote(part.at[k // 2, core, two], inbox.at[k // 2, two], way, lane, index))

    def wait_recv(copy):
        copy.wait_recv()

    def sent(act, code, index, way):
        message(act, code, index, way, sent_by[way], way == IN, way == OUT)

    def start(copy):
        copy.start()

    def wait_send(copy):
        copy.wait_send()

    def counted(n, code):
        return (n + jnp.where(code < NONE, 1, 0)) % RING

    mid_at, mid_whole, mid_blocks = plan(True)
    end_at, end_whole, end_blocks = plan(False)
    assert all(MID_OUT.index(SUMS + 2 * j) >= r + SUM_LAG for j, r in enumerate(mid_blocks))
    assert len(set(end_blocks)) == BLOCKS

    def count_of(at):
        return [sum(s <= r for s, _ in at) for r in range(ROUNDS)]

    def units(r):
        return pick(mid, r, count_of(mid_at), count_of(end_at))

    def which(r, blocks, here):
        found = BLOCKS
        for j, s in enumerate(blocks):
            found = jnp.where(r == s, j, found)
        return jnp.where(here, found, BLOCKS)

    def multiply(left, column, first, deep):
        for start in range(0, columns, 256):
            cut = slice(start, min(start + 256, columns))
            total[column, :, cut] += jnp.dot(
                left, amps[pl.ds(first, deep), cut], preferred_element_type=jnp.float32
            )

    def product(code):
        column, c = turned(code // 8), code % 8
        mine = pl.ds(pl.multiple_of(column * 4 * rows, 4 * rows), 4 * rows)

        @pl.when(c < HELPED)
        def _():
            first = pl.multiple_of(c * deep_helped, 128)
            multiply(helped[c, mine, :], column, first, deep_helped)

        @pl.when(c >= HELPED)
        def _():
            first = pl.multiple_of(deep_all_helped + (c - HELPED) * deep_plain, 128)
            multiply(plain[c - HELPED, mine, :], column, first, deep_plain)

    def exchange(j):
        return pltpu.make_async_remote_copy(
            src_ref=part.at[j, 1 - core],
            dst_ref=inbox.at[j],
            send_sem=part_send.at[j % 2],
            recv_sem=part_recv.at[j % 2],
            device_id=(me, 1 - core),
            device_id_type=MESH,
        )

    def lend(j):
        sums = jnp.dot(helped[0], lent[j, :deep_helped, :], preferred_element_type=jnp.float32)
        for c in range(1, HELPED):
            deep = slice(c * deep_helped, (c + 1) * deep_helped)
            sums += jnp.dot(helped[c], lent[j, deep, :], preferred_element_type=jnp.float32)
        for k in range(4):
            for h in range(2):
                first = (2 * k + h) * half
                part[j, h, k] = sums[first : first + half]
        exchange(j).start()

    def join(j):
        exchange(j).wait()
        part[j, core] += inbox[j]

    def take(j):
        mine = pl.ds(pl.multiple_of(core * half, half), half)
        total[:, mine, pl.ds(pl.multiple_of(j * 128, 128), 128)] += inbox[j]

    def hand_over(column):
        return pltpu.make_async_remote_copy(
            src_ref=total.at[column, pl.ds(pl.multiple_of((1 - core) * half, half), half), :],
            dst_ref=other.at[column],
            send_sem=col_send.at[column],
            recv_sem=col_recv.at[column],
            device_id=(me, 1 - core),
            device_id_type=MESH,
        )

    def finish(column):
        hand_over(column).wait()
        mine = total[column, pl.ds(pl.multiple_of(core * half, half), half), :] + other[column]
        for k in range(2):
            start = pl.multiple_of((k * 4 + column) * rows, rows)
            out_ref[pl.ds(start, rows), :] = mine[k * rows : (k + 1) * rows].astype(out_ref.dtype)

    pl.semaphore_wait(barrier, jnp.where(mid, 5, 4))
    for c in range(CHUNKS):
        load(c).wait()

    ways_out = [(coded(MID[way]), coded(END[way])) for way in range(WAYS)]
    ways_in = [(coded(MID_FROM[way]), coded(END_FROM[way])) for way in range(WAYS)]

    def said_by(r, way):
        code = either(*(table[r] if r < len(table) else NONE for table in ways_out[way]))
        return code, either(number(MID[way], r), number(END[way], r))

    for r in range(FIRST):
        for way in range(WAYS):
            sent(start, *said_by(r, way), way)
    load_amps[1].start()

    @pl.when(mid)
    def _():
        load_amps[0].start()

    total[...] = jnp.zeros_like(total)

    def step(r, carry):
        n_in, n_out, history = carry
        after_in, after_out, now = [], [], []
        for way in range(WAYS):
            code = pick(mid, r, *ways_in[way])
            message(wait_recv, code, n_in[way], way, come_by[way], way == OUT, way == IN)
            after_in.append(counted(n_in[way], code))

        joined = which(r - SUM_LAG, mid_blocks, mid)

        @pl.when(joined < BLOCKS)
        def _():
            join(joined)

        for way in range(WAYS):
            code = pick(mid, r, *ways_out[way])
            sent(start, code, n_out[way], way)
            now.append((code, n_out[way]))
            after_out.append(counted(n_out[way], code))
        for way in range(WAYS):
            sent(wait_send, *history[0][way], way)

        @pl.when(r == AMPS_THERE)
        def _():
            load_amps[1].wait()

            @pl.when(mid)
            def _():
                load_amps[0].wait()

        lending = which(r, mid_blocks, mid)

        @pl.when(lending < BLOCKS)
        def _():
            lend(lending)

        def unit(u, _):
            product(pick(mid, u, *([code // CHUNKS * 8 + code % CHUNKS for _, code in at] for at in (mid_at, end_at))))
            for q in range(4):

                @pl.when(u == jnp.where(mid, mid_whole[q], end_whole[q]))
                def _():
                    hand_over(turned(q)).start()

            return 0

        lax.fori_loop(units(r - 1), units(r), unit, 0)

        taken = which(r, end_blocks, jnp.logical_not(mid))

        @pl.when(taken < BLOCKS)
        def _():
            take(taken)

        return after_in, after_out, (*history[1:], now)

    nothing = (jnp.int32(NONE), jnp.int32(0))
    counts = [either(number(MID[way], FIRST), number(END[way], FIRST)) for way in range(WAYS)]
    history = [[nothing] * WAYS] * (SENT_LAG - FIRST)
    history += [[said_by(r, way) for way in range(WAYS)] for r in range(FIRST)]
    first = jax.tree.map(jnp.int32, ([0] * WAYS, counts, tuple(history)))
    lax.fori_loop(FIRST, ROUNDS, step, first)
    for r in range(ROUNDS - SENT_LAG, SENDS):
        for way in range(WAYS):
            if any(r < len(table) and table[r] < NONE for table in ways_out[way]):
                sent(wait_send, *said_by(r, way), way)
    orders = [sorted(range(4), key=lambda q: whole[q]) for whole in (mid_whole, end_whole)]
    for of_mid, of_end in zip(*orders):
        finish(turned(jnp.where(mid, of_mid, of_end)))


def linked(tamps, integrals):
    rows, depth = integrals.shape
    columns = tamps.shape[1]
    return pl.pallas_call(
        kernel,
        out_shape=pltpu.VMEM((8 * rows, columns), jnp.bfloat16),
        in_specs=[pl.BlockSpec(memory_space=pl.ANY)] * 2,
        out_specs=pl.BlockSpec(memory_space=pltpu.VMEM),
        scratch_shapes=[
            pltpu.VMEM((HELPED, 16 * rows, HELPED_WIDE * 128), jnp.bfloat16),
            pltpu.VMEM((PLAIN, 16 * rows, PLAIN_WIDE * 128), jnp.bfloat16),
            pltpu.VMEM((depth, columns), jnp.bfloat16),
            pltpu.VMEM((BLOCKS, HELPED * HELPED_WIDE * 128, 128), jnp.bfloat16),
            pltpu.VMEM((4, 4 * rows, columns), jnp.float32),
            pltpu.VMEM((4, 2 * rows, columns), jnp.float32),
            pltpu.VMEM((BLOCKS, 2, 4, 2 * rows, 128), jnp.float32),
            pltpu.VMEM((BLOCKS, 4, 2 * rows, 128), jnp.float32),
            pltpu.SemaphoreType.DMA((4, RING)),
            pltpu.SemaphoreType.DMA((4, RING)),
            pltpu.SemaphoreType.DMA((CHUNKS,)),
            pltpu.SemaphoreType.DMA((2,)),
            pltpu.SemaphoreType.DMA((4,)),
            pltpu.SemaphoreType.DMA((4,)),
            pltpu.SemaphoreType.DMA((2,)),
            pltpu.SemaphoreType.DMA((2,)),
        ],
        compiler_params=pltpu.CompilerParams(
            collective_id=0, has_side_effects=True, vmem_limit_bytes=56 * 2**20
        ),
    )(tamps, integrals)


def shards(tamps, integrals):
    gathered = lax.all_gather(integrals, "con", axis=0, tiled=True)
    partial_value = jnp.dot(gathered, tamps, preferred_element_type=jnp.float32)
    summed = lax.psum_scatter(partial_value, "rep", scatter_dimension=0, tiled=True)
    return summed.astype(jnp.bfloat16)


def solution(mesh):
    in_specs = (P("rep", "con"), P("con", "rep"))
    out_specs = P("rep", "con")
    part = linked if (mesh.shape["con"], mesh.shape["rep"]) == (16, 2) else shards
    return jax.shard_map(part, mesh=mesh, in_specs=in_specs, out_specs=out_specs, check_vma=False)
```

```python
import functools

import jax
import jax.numpy as jnp
from jax import lax
from jax.experimental import pallas as pl
from jax.experimental.pallas import tpu as pltpu
from jax.sharding import PartitionSpec as P

MESH = pl.DeviceIdType.MESH

HELPED, PLAIN = 2, 5
HELPED_WIDE, PLAIN_WIDE = 7, 10
CHUNKS = HELPED + PLAIN
PER_BLOCK = 4
BLOCKS = 7
SENT_LAG = 4
AMPS_THERE = 5
FIRST = 3
RING = 8
ROUND_US = 3.5
UNIT_US = 0.85
LEND_US = 1.1
SUM_LAG = 1
PIECES = 16 * CHUNKS
WAYS = 4
AMPS = PIECES
SUMS = AMPS + BLOCKS * PER_BLOCK

END_X = (
    3, 4, 5, -1, 59, 60, -1, 9, 65, -1, 18, 6, 20, -1, 66, 76, -1, 102, 69, -1, 81, 19, 23, -1, 17,
    27, -1, 79, 75, -1, 54, 11, 10, -1, 110, 16, -1, 24, 72, -1, 80,
)
END_Y = (
    3, 4, 2, -1, 9, 5, -1, 33, 6, -1, 10, 13, 12, -1, 46, 75, -1, 40, 86, -1, 27, 81, 97, -1, 23,
    34, -1, 45, 109, -1, 54, 55, 16, -1, 17, 39, -1, 24, 11,
)
END_IN = (
    1, 112, 0, 4, 6, 113, 114, 58, -1, 115, 116, 117, 118, 119, 31, 89, -1, 120, 121, 122, 123, 124,
    125, 126, 127, 128, 129, 130, 131, 132, 133, 134, 135, 136, 137, 138, 139, 73, 45, -1, 101,
)
MID_X = (
    8, 7, 12, 14, 64, 0, 4, 70, 57, 6, -1, 58, 78, 49, 76, -1, 56, 31, 23, -1, 25, 68, 18, -1, 97,
    79, -1, 54, 60, -1, 83, 16, 110, -1, 72, 10, -1, 95, 65, -1, 66,
)
MID_Y = (
    7, 8, 12, 1, 35, 0, 20, 4, -1, 22, 99, 58, 49, 85, 75, -1, 106, 81, 104, -1, 89, 23, 6, -1, 53,
    47, -1, 46, 54, -1, 16, 39, 18, -1, 24, 86, -1, 10, 31, -1, 52,
)
MID_OUT = (
    9, 12, 11, -1, 18, 10, -1, 13, 20, -1, 76, 75, 40, -1, 86, 81, -1, 27, 23, -1, 17, 140, 141,
    142, 143, -1, 144, 54, 16, -1, 145, 146, 147, 24, 148, -1, 149, 150, 151, -1, 152, 153,
)
MID_IN = (
    7, 11, 13, 63, 1, 68, -1, 92, 28, 8, 64, 56, 60, 6, -1, 2, 10, -1, 31, 104, 40, -1, 48, 33, -1,
    9, 62, -1, 46, 3, 26, -1, 34, 111, -1, 72, 82, -1, 44, 80,
)
END_FROM_X = (
    -1, -1, -1, 31, -1, 32, 33, 87, -1, 88, 37, -1, 93, 46, -1, 34, 48, 94, -1, 104, 74, -1, 97,
    109, -1, 47, 51, 45, -1, 55, 107, -1, 103, 26, -1, 39, 38, 82, -1, 44, 52, -1, 100, 108,
)
END_FROM_Y = (
    -1, -1, -1, 59, -1, 60, 58, 65, -1, 61, 89, -1, 62, 66, -1, 69, 68, 102, -1, 19, 96, -1, 30, 83,
    -1, 25, 41, 79, -1, 90, 101, -1, 53, 110, -1, 111, 72, 73, -1, 95, 80, -1, 67,
)
END_FROM_MID = (
    -1, -1, -1, 9, -1, 12, 11, 18, -1, 10, 13, -1, 20, 76, -1, 75, 40, 86, -1, 81, 27, -1, 23, 17,
    140, 141, -1, 142, 143, 144, 54, -1, 16, 145, 146, 147, -1, 24, 148, 149, 150, 151, -1, 152, 153,
)
MID_FROM_X = (
    -1, -1, -1, 36, 35, 40, 42, 92, 28, -1, 32, 98, 85, 34, 86, 106, 21, -1, 104, 84, 3, -1, 51, 53,
    -1, 96, 46, 69, -1, 107, 26, -1, 88, 111, -1, 44, 82, 100, -1, 38, 67, -1, 93, 94,
)
MID_FROM_Y = (
    -1, -1, -1, 63, 64, 68, 57, 91, 56, -1, 76, 60, 78, 43, 2, 105, 29, -1, 19, 50, 25, -1, 48, 33,
    -1, 79, 62, 109, -1, 103, 102, -1, 110, 72, -1, 95, 74, 80, -1, 30, 66, -1, 87, 108,
)
MID_FROM_MID = (
    -1, -1, -1, 14, 18, -1, 20, 70, 22, 75, 99, 49, 15, 71, 77, 81, -1, 27, 23, -1, 17, 52, -1, 97,
    47, 41, -1, 54, 16, -1, 83, 39, -1, 24, 5, 55, -1, 90, 65, -1, 61, 37, -1, 59,
)
MID_FROM_END = (
    -1, -1, -1, 1, 112, 0, 4, -1, 6, 113, 114, 58, 115, 116, 117, 118, 119, 31, -1, 89, 120, 121,
    122, 123, 124, 125, 126, 127, 128, 129, 130, 131, 132, 133, 134, 135, 136, 137, 138, 139, 73,
    -1, 45, 101,
)
END = (END_X, END_Y, END_IN, (-1,))
MID = (MID_X, MID_Y, MID_IN, MID_OUT)
END_FROM = (END_FROM_X, END_FROM_Y, END_FROM_MID, (-1,))
MID_FROM = (MID_FROM_X, MID_FROM_Y, MID_FROM_MID, MID_FROM_END)
SENDS = max(map(len, END + MID))
ROUNDS = max(map(len, END_FROM + MID_FROM))
X, Y, IN, OUT = range(4)
NONE = 255


def parts(code):
    return code // CHUNKS // 4, code // CHUNKS % 4, code % CHUNKS


def arrivals(mid):
    there = {(0, 1 if mid else 0, c): 0 for c in range(CHUNKS)}
    amps, sums = {}, {}
    for table in MID_FROM if mid else END_FROM:
        for r, code in enumerate(table):
            if 0 <= code < PIECES:
                there[parts(code)] = r
            elif AMPS <= code < SUMS:
                amps[(code - AMPS) // PER_BLOCK] = r
            elif code >= SUMS:
                sums[(code - SUMS) // 2] = r
    return there, amps, sums


def plan(mid):
    there, amps, sums = arrivals(mid)
    ready = []
    for q in range(4):
        for c in range(0 if mid else HELPED, CHUNKS):
            ready.append((max(there[q, p, c] for p in range(4)), q, c))
    ready.sort()
    helped_there = max(there[q, p, c] for q in range(4) for p in range(4) for c in range(HELPED)) if mid else 0
    blocks = []
    for j in range(BLOCKS):
        if mid:
            blocks.append(max(amps[j], helped_there, blocks[-1] + 1 if j else 0))
        else:
            blocks.append(sums[j])
    at, credit = [], 0.0
    for r in range(AMPS_THERE, ROUNDS):
        credit = min(credit + ROUND_US, ROUND_US) - LEND_US * blocks.count(r) * mid
        while ready and ready[0][0] <= r and (credit > 0 or r == ROUNDS - 1):
            _, q, c = ready.pop(0)
            at.append((r, q * CHUNKS + c))
            credit -= UNIT_US
    whole = [max(u for u, (_, code) in enumerate(at) if code // CHUNKS == q) for q in range(4)]
    return at, whole, blocks


def chosen(index, values):
    while len(values) > 1:
        odd = index % 2 == 1
        index = index // 2
        pairs = [values[i : i + 2] for i in range(0, len(values), 2)]
        values = [jnp.where(odd, v[1], v[0]) if len(v) == 2 else v[0] for v in pairs]
    return values[0]


def pick(mid, index, of_mid, of_end):
    size = ROUNDS + -ROUNDS % 3
    words = []
    for table in (of_mid, of_end):
        full = [NONE if v < 0 else v for v in table] + [NONE] * (size - len(table))
        words.append([full[i] + 256 * full[i + 1] + 65536 * full[i + 2] for i in range(0, size, 3)])
    word = chosen(index // 3, [a if a == b else jnp.where(mid, a, b) for a, b in zip(*words)])
    digit = index % 3
    shifted = jnp.where(digit == 0, word, jnp.where(digit == 1, word // 256, word // 65536))
    return shifted % 256


def number(table, r):
    return sum(code >= 0 for code in table[:r]) % RING


def kernel(
    tamps_hbm, slab_hbm, out_ref, helped, plain, amps, lent, total, other, part, inbox,
    send_sem, recv_sem, own_sem, amps_sem, col_send, col_recv, part_send, part_recv,
):
    me = lax.axis_index("con")
    core = lax.axis_index("rep")
    z, y, x = me // 4, (me // 2) % 2, me % 2
    rows = slab_hbm.shape[0]
    columns = amps.shape[1]
    half = 2 * rows
    own = y * 2 + x
    low = z < 2
    mid = jnp.logical_and(z > 0, z < 3)
    deep_helped, deep_plain = HELPED_WIDE * 128, PLAIN_WIDE * 128
    deep_all_helped = HELPED * deep_helped
    deep_part = deep_all_helped // PER_BLOCK

    def turned(q):
        qx, qy = q % 2, q // 2
        return (y + qy - 2 * y * qy) * 2 + (x + qx - 2 * x * qx)

    neighbour = (
        z * 4 + y * 2 + 1 - x,
        z * 4 + (1 - y) * 2 + x,
        jnp.where(low, me + 4, me - 4),
        jnp.where(low, me - 4, me + 4),
    )
    up, down = jnp.where(low, 2, 3), jnp.where(low, 3, 2)
    sent_by, come_by = (0, 1, up, down), (0, 1, down, up)

    load_amps = [
        pltpu.make_async_copy(
            tamps_hbm.at[pl.ds(first, count), :], amps.at[pl.ds(first, count), :], amps_sem.at[k]
        )
        for k, (first, count) in enumerate(
            ((0, deep_all_helped), (deep_all_helped, PLAIN * deep_plain))
        )
    ]

    def load(c):
        here = pl.ds(pl.multiple_of((own * 4 + z) * rows, rows), rows)
        if c < HELPED:
            cut = slice(c * deep_helped, (c + 1) * deep_helped)
            return pltpu.make_async_copy(slab_hbm.at[:, cut], helped.at[c, here, :], own_sem.at[c])
        first = deep_all_helped + (c - HELPED) * deep_plain
        cut = slice(first, first + deep_plain)
        return pltpu.make_async_copy(slab_hbm.at[:, cut], plain.at[c - HELPED, here, :], own_sem.at[c])

    barrier = pltpu.get_barrier_semaphore()
    for way in (X, Y, IN):
        pl.semaphore_signal(barrier, inc=1, device_id=(neighbour[way], core), device_id_type=MESH)
    pl.semaphore_signal(barrier, inc=1, device_id=(me, 1 - core), device_id_type=MESH)

    @pl.when(mid)
    def _():
        pl.semaphore_signal(barrier, inc=1, device_id=(neighbour[OUT], core), device_id_type=MESH)

    for c in range(CHUNKS):
        load(c).start()
    def coded(table):
        out = []
        for code in table:
            if code < 0:
                out.append(NONE)
            elif code >= SUMS:
                out.append(160 + code - SUMS)
            elif code >= AMPS:
                out.append(128 + code - AMPS)
            else:
                q, p, c = parts(code)
                out.append((q * 4 + p) * 8 + c)
        return out

    def either(of_mid, of_end):
        if isinstance(of_mid, int) and isinstance(of_end, int) and of_mid == of_end:
            return of_mid
        return jnp.where(mid, of_mid, of_end)

    def remote(src, dst, way, lane, index):
        return pltpu.make_async_remote_copy(
            src_ref=src,
            dst_ref=dst,
            send_sem=send_sem.at[way, index],
            recv_sem=recv_sem.at[lane, index],
            device_id=(neighbour[way], core),
            device_id_type=MESH,
        )

    def message(act, code, index, way, lane, amps_too, sums_too):
        q, p, c = code // 32, code // 8 % 4, code % 8
        place = turned(q) * 4 + jnp.where(low, p, 3 - p)
        mine = pl.ds(pl.multiple_of(place * rows, rows), rows)

        @pl.when(jnp.logical_and(code < 128, c < HELPED))
        def _():
            piece = helped.at[c, mine, :]
            act(remote(piece, piece, way, lane, index))

        @pl.when(jnp.logical_and(code < 128, c >= HELPED))
        def _():
            piece = plain.at[c - HELPED, mine, :]
            act(remote(piece, piece, way, lane, index))

        if amps_too:

            @pl.when(jnp.logical_and(code >= 128, code < 160))
            def _():
                k = code - 128
                j = k // PER_BLOCK
                deep = pl.ds(pl.multiple_of(k % PER_BLOCK * deep_part, deep_part), deep_part)
                cut = pl.ds(pl.multiple_of(j * 128, 128), 128)
                act(remote(tamps_hbm.at[deep, cut], lent.at[j, deep, :], way, lane, index))

        if sums_too:

            @pl.when(jnp.logical_and(code >= 160, code < NONE))
            def _():
                k = code - 160
                two = pl.ds(k % 2 * 2, 2)
                act(remote(part.at[k // 2, core, two], inbox.at[k // 2, two], way, lane, index))

    def wait_recv(copy):
        copy.wait_recv()

    def sent(act, code, index, way):
        message(act, code, index, way, sent_by[way], way == IN, way == OUT)

    def start(copy):
        copy.start()

    def wait_send(copy):
        copy.wait_send()

    def counted(n, code):
        return (n + jnp.where(code < NONE, 1, 0)) % RING

    mid_at, mid_whole, mid_blocks = plan(True)
    end_at, end_whole, end_blocks = plan(False)
    assert all(MID_OUT.index(SUMS + 2 * j) >= r + SUM_LAG for j, r in enumerate(mid_blocks))
    assert len(set(end_blocks)) == BLOCKS

    def count_of(at):
        return [sum(s <= r for s, _ in at) for r in range(ROUNDS)]

    def units(r):
        return pick(mid, r, count_of(mid_at), count_of(end_at))

    def which(r, blocks, here):
        found = BLOCKS
        for j, s in enumerate(blocks):
            found = jnp.where(r == s, j, found)
        return jnp.where(here, found, BLOCKS)

    def multiply(left, column, first, deep):
        for start in range(0, columns, 256):
            cut = slice(start, min(start + 256, columns))
            total[column, :, cut] += jnp.dot(
                left, amps[pl.ds(first, deep), cut], preferred_element_type=jnp.float32
            )

    def product(code):
        column, c = turned(code // 8), code % 8
        mine = pl.ds(pl.multiple_of(column * 4 * rows, 4 * rows), 4 * rows)

        @pl.when(c < HELPED)
        def _():
            first = pl.multiple_of(c * deep_helped, 128)
            multiply(helped[c, mine, :], column, first, deep_helped)

        @pl.when(c >= HELPED)
        def _():
            first = pl.multiple_of(deep_all_helped + (c - HELPED) * deep_plain, 128)
            multiply(plain[c - HELPED, mine, :], column, first, deep_plain)

    def exchange(j):
        return pltpu.make_async_remote_copy(
            src_ref=part.at[j, 1 - core],
            dst_ref=inbox.at[j],
            send_sem=part_send.at[j % 2],
            recv_sem=part_recv.at[j % 2],
            device_id=(me, 1 - core),
            device_id_type=MESH,
        )

    def lend(j):
        sums = jnp.dot(helped[0], lent[j, :deep_helped, :], preferred_element_type=jnp.float32)
        for c in range(1, HELPED):
            deep = slice(c * deep_helped, (c + 1) * deep_helped)
            sums += jnp.dot(helped[c], lent[j, deep, :], preferred_element_type=jnp.float32)
        for k in range(4):
            for h in range(2):
                first = (2 * k + h) * half
                part[j, h, k] = sums[first : first + half]
        exchange(j).start()

    def join(j):
        exchange(j).wait()
        part[j, core] += inbox[j]

    def take(j):
        mine = pl.ds(pl.multiple_of(core * half, half), half)
        total[:, mine, pl.ds(pl.multiple_of(j * 128, 128), 128)] += inbox[j]

    def hand_over(column):
        return pltpu.make_async_remote_copy(
            src_ref=total.at[column, pl.ds(pl.multiple_of((1 - core) * half, half), half), :],
            dst_ref=other.at[column],
            send_sem=col_send.at[column],
            recv_sem=col_recv.at[column],
            device_id=(me, 1 - core),
            device_id_type=MESH,
        )

    def finish(column):
        hand_over(column).wait()
        mine = total[column, pl.ds(pl.multiple_of(core * half, half), half), :] + other[column]
        for k in range(2):
            start = pl.multiple_of((k * 4 + column) * rows, rows)
            out_ref[pl.ds(start, rows), :] = mine[k * rows : (k + 1) * rows].astype(out_ref.dtype)

    pl.semaphore_wait(barrier, jnp.where(mid, 5, 4))
    for c in range(CHUNKS):
        load(c).wait()

    ways_out = [(coded(MID[way]), coded(END[way])) for way in range(WAYS)]
    ways_in = [(coded(MID_FROM[way]), coded(END_FROM[way])) for way in range(WAYS)]

    def said_by(r, way):
        code = either(*(table[r] if r < len(table) else NONE for table in ways_out[way]))
        return code, either(number(MID[way], r), number(END[way], r))

    for r in range(FIRST):
        for way in range(WAYS):
            sent(start, *said_by(r, way), way)
    load_amps[1].start()

    @pl.when(mid)
    def _():
        load_amps[0].start()

    total[...] = jnp.zeros_like(total)

    def step(r, carry):
        n_in, n_out, history = carry
        after_in, after_out, now = [], [], []
        for way in range(WAYS):
            code = pick(mid, r, *ways_in[way])
            message(wait_recv, code, n_in[way], way, come_by[way], way == OUT, way == IN)
            after_in.append(counted(n_in[way], code))

        joined = which(r - SUM_LAG, mid_blocks, mid)

        @pl.when(joined < BLOCKS)
        def _():
            join(joined)

        for way in range(WAYS):
            code = pick(mid, r, *ways_out[way])
            sent(start, code, n_out[way], way)
            now.append((code, n_out[way]))
            after_out.append(counted(n_out[way], code))
        for way in range(WAYS):
            sent(wait_send, *history[0][way], way)

        @pl.when(r == AMPS_THERE)
        def _():
            load_amps[1].wait()

            @pl.when(mid)
            def _():
                load_amps[0].wait()

        lending = which(r, mid_blocks, mid)

        @pl.when(lending < BLOCKS)
        def _():
            lend(lending)

        def unit(u, _):
            product(pick(mid, u, *([code // CHUNKS * 8 + code % CHUNKS for _, code in at] for at in (mid_at, end_at))))
            for q in range(4):

                @pl.when(u == jnp.where(mid, mid_whole[q], end_whole[q]))
                def _():
                    hand_over(turned(q)).start()

            return 0

        lax.fori_loop(units(r - 1), units(r), unit, 0)

        taken = which(r, end_blocks, jnp.logical_not(mid))

        @pl.when(taken < BLOCKS)
        def _():
            take(taken)

        return after_in, after_out, (*history[1:], now)

    nothing = (jnp.int32(NONE), jnp.int32(0))
    counts = [either(number(MID[way], FIRST), number(END[way], FIRST)) for way in range(WAYS)]
    history = [[nothing] * WAYS] * (SENT_LAG - FIRST)
    history += [[said_by(r, way) for way in range(WAYS)] for r in range(FIRST)]
    first = jax.tree.map(jnp.int32, ([0] * WAYS, counts, tuple(history)))
    lax.fori_loop(FIRST, ROUNDS, step, first)
    for r in range(ROUNDS - SENT_LAG, SENDS):
        for way in range(WAYS):
            if any(r < len(table) and table[r] < NONE for table in ways_out[way]):
                sent(wait_send, *said_by(r, way), way)
    orders = [sorted(range(4), key=lambda q: whole[q]) for whole in (mid_whole, end_whole)]
    for of_mid, of_end in zip(*orders):
        finish(turned(jnp.where(mid, of_mid, of_end)))


def linked(tamps, integrals):
    rows, depth = integrals.shape
    columns = tamps.shape[1]
    return pl.pallas_call(
        kernel,
        out_shape=pltpu.VMEM((8 * rows, columns), jnp.bfloat16),
        in_specs=[pl.BlockSpec(memory_space=pl.ANY)] * 2,
        out_specs=pl.BlockSpec(memory_space=pltpu.VMEM),
        scratch_shapes=[
            pltpu.VMEM((HELPED, 16 * rows, HELPED_WIDE * 128), jnp.bfloat16),
            pltpu.VMEM((PLAIN, 16 * rows, PLAIN_WIDE * 128), jnp.bfloat16),
            pltpu.VMEM((depth, columns), jnp.bfloat16),
            pltpu.VMEM((BLOCKS, HELPED * HELPED_WIDE * 128, 128), jnp.bfloat16),
            pltpu.VMEM((4, 4 * rows, columns), jnp.float32),
            pltpu.VMEM((4, 2 * rows, columns), jnp.float32),
            pltpu.VMEM((BLOCKS, 2, 4, 2 * rows, 128), jnp.float32),
            pltpu.VMEM((BLOCKS, 4, 2 * rows, 128), jnp.float32),
            pltpu.SemaphoreType.DMA((4, RING)),
            pltpu.SemaphoreType.DMA((4, RING)),
            pltpu.SemaphoreType.DMA((CHUNKS,)),
            pltpu.SemaphoreType.DMA((2,)),
            pltpu.SemaphoreType.DMA((4,)),
            pltpu.SemaphoreType.DMA((4,)),
            pltpu.SemaphoreType.DMA((2,)),
            pltpu.SemaphoreType.DMA((2,)),
        ],
        compiler_params=pltpu.CompilerParams(
            collective_id=0, has_side_effects=True, vmem_limit_bytes=56 * 2**20
        ),
    )(tamps, integrals)


def shards(tamps, integrals):
    gathered = lax.all_gather(integrals, "con", axis=0, tiled=True)
    partial_value = jnp.dot(gathered, tamps, preferred_element_type=jnp.float32)
    summed = lax.psum_scatter(partial_value, "rep", scatter_dimension=0, tiled=True)
    return summed.astype(jnp.bfloat16)


def solution(mesh):
    in_specs = (P("rep", "con"), P("con", "rep"))
    out_specs = P("rep", "con")
    part = linked if (mesh.shape["con"], mesh.shape["rep"]) == (16, 2) else shards
    return jax.shard_map(part, mesh=mesh, in_specs=in_specs, out_specs=out_specs, check_vma=False)
```
